128 devices in a mesh: group: 2 (over y_lo), seq: 8 (over y_hi, z), mp: 8 (over x, core).
Axes of the slice: x: 4, y: 4 (y_hi: 2, y_lo: 2; y = y_hi * 2 + y_lo), z: 4, core: 2. Of those that a mesh axis runs over, the one named last changes fastest.
Arguments:
- embeds: bfloat16 [16384, 8192], P('seq', 'mp'), may hold values from -250 to 250
- image_feats: bfloat16 [1024, 7296], P('seq'), may hold values from -6 to 6
- image_pos: int32 [1024], P('seq'), may hold values from 0 to 16383, as said below
- proj_w: bfloat16 [7296, 8192], P('seq', 'mp'), may hold values from -0.0625 to 0.0625
- proj_b: bfloat16 [8192], P('mp'), may hold values from -3 to 3
- norm_gain: bfloat16 [8192], P('mp'), may hold values from 0.099609375 to 1.8984375
- kv_w: bfloat16 [8192, 2048], P('mp'), may hold values from -0.0625 to 0.0625
- prompt_lengths: int32 [4], replicated, may hold values from 2048 to 4096
- page_owner: int32 [1024, 1], P('seq'), may hold values from 0 to 7; in each aligned block of 128 rows (0 to 127, 128 to 255, ...) at most 32 rows name the same one
- queries: bfloat16 [1024, 8192], P('seq', 'mp'), may hold values from -180 to 180
- kv_cache: bfloat16 [1024, 128, 2048], P('seq', None, 'mp'), may hold values from -5 to 5
- new_kv: bfloat16 [1024, 2048], P('seq', 'mp'), may hold values from -5 to 5
- cache_lengths: int32 [1024], P('seq'), may hold values from 2 to 128
Outputs:
- page_slots: bfloat16 [4096, 16, 2048], P(('group', 'seq'), None, 'mp')
- row_states: bfloat16 [2048, 8192], P(('group', 'seq'), 'mp')
The draws below stay inside these ranges and needn't reach their ends.
Inputs may be any that keep to these rules, and one draw needn't show every extreme that they name: `image_pos`: distinct and increasing; entries s * 128 to (s + 1) * 128 - 1 lie among tokens s * 2048 to (s + 1) * 2048 - 1. `page_owner`: among the 128 pages of one seq index no owner is named more than 32 times.
All inputs are finite; a program needn't handle non-finite values.
Results may differ from the reference program's by a relative error of at most 0.005.
Values may be sent and summed in bfloat16 or wider, within the bound.
No kernel may reach another device: no remote copies, remote signals or barrier semaphores. Data moves between devices by JAX's collectives and lax.ppermute only.
A program may use at most 128 MiB of HBM per device.

```python
import math
import jax
import jax.numpy as jnp
import numpy as np
from jax import lax

D = 8192
QH = 64
KVH = 8
HEAD = 128
C_VIS = 7296
PAGE = 16
PROMPT_LEN = 4096
ROWS_DEV = 2048
BATCH_DEV = 128
CACHE = 128
TOKENS = 16384
IMGS = 1024
PROMPTS = 4
PAGES_DEV = 128
PAGES = 1024
CAP = 32
N_SEQ = 8


def decode_pair(key):
    cache_key = jax.random.fold_in(key, 11)
    query_key = jax.random.fold_in(key, 12)
    stored = jnp.clip(jax.random.normal(cache_key, (IMGS, CACHE, KVH, 2, HEAD), jnp.float32), -5.0, 5.0)
    asked = jnp.clip(jax.random.normal(query_key, (IMGS, KVH, QH // KVH, HEAD), jnp.float32), -5.0, 5.0)
    return (stored.reshape(IMGS, CACHE, KVH * 2 * HEAD), asked.reshape(IMGS, QH * HEAD))


def draw_kv_cache(key, part):
    return decode_pair(key)[0].astype(jnp.bfloat16)


def draw_queries(key, part):
    return decode_pair(key)[1].astype(jnp.bfloat16)


def draw_embeds(key, part):
    row_u = jax.random.uniform(jax.random.fold_in(key, 22), (TOKENS, 1), jnp.float32)
    col_u = jax.random.uniform(jax.random.fold_in(key, 23), (1, D), jnp.float32)
    trend = jnp.arange(D, dtype=jnp.float32)[None, :] / D
    base = jnp.clip(jax.random.normal(jax.random.fold_in(key, 21), (TOKENS, D), jnp.float32), -6.0, 6.0)
    col_scale = 10.0 ** (0.5 * trend + 0.5 * col_u)
    row_scale = 10.0 ** (row_u - 0.5)
    return (base * row_scale * col_scale).astype(jnp.bfloat16)


def draw_image_pos(key, part):

    def one_shard(shard):
        order = jax.random.permutation(jax.random.fold_in(key, 31 + shard), ROWS_DEV)
        picked = jnp.sort(order[:BATCH_DEV])
        return picked.astype(jnp.int32) + shard * ROWS_DEV
    shards = jnp.arange(IMGS // BATCH_DEV, dtype=jnp.int32)
    return jax.vmap(one_shard)(shards).reshape(IMGS).astype(jnp.int32)


def set_ends(array, key, least, largest):
    spot = [jax.random.randint(jax.random.fold_in(key, axis), (), 0, length) for axis, length in enumerate(array.shape)]
    widest = array.shape.index(max(array.shape))
    neighbour = spot[:widest] + [(spot[widest] + 1) % array.shape[widest]] + spot[widest + 1:]
    return array.at[tuple(spot)].set(least).at[tuple(neighbour)].set(largest)


def level_of(stream_key, dims, split, low, largest):
    loudness = 1.0
    for dim, blocks in split:
        draws = jax.random.uniform(jax.random.fold_in(jax.random.fold_in(stream_key, 6), dim), (blocks,), jnp.float32, low / len(split), largest / len(split))
        loudness = loudness * jnp.repeat(jnp.exp(draws), dims[dim] // blocks).reshape((-1,) + (1,) * (len(dims) - 1 - dim))
    return loudness


def assign_block(own_key, own, number, rows, number_of, top, bound, skew):
    sequence = jax.random.permutation(own_key, number_of)
    crowded, usual = load_shares(number_of, rows * top, bound, skew, True), load_shares(number_of, rows * top, bound, skew, False)
    places = jnp.arange(number_of)

    def named(tallies, rotation):
        used = int((tallies > 0).sum())
        fixed = max(1, used // 4)
        shifted = fixed + (places - fixed + rotation * (used - fixed)) % max(1, number_of - fixed)
        return jnp.zeros((number_of,), jnp.int32).at[sequence[jnp.where(places < fixed, places, shifted)]].set(jnp.asarray(tallies, jnp.int32))

    tallies = jnp.where(number % 4 == 0, named(crowded, number // 4), named(usual, number - number // 4 - 1))
    mixed = jax.random.permutation(jax.random.fold_in(own, 3), number_of)
    giver, sink = mixed[0:number_of // 2 * 2:2], mixed[1:number_of // 2 * 2:2]
    slack = jnp.minimum(tallies[giver] - 1, bound - tallies[sink]) // 2
    slack = jnp.where((giver == sequence[0]) | (sink == sequence[0]) | (tallies[sink] == 0), 0, jnp.maximum(slack, 0))
    shifted = jax.random.randint(jax.random.fold_in(own, 4), (number_of // 2,), 0, 1 << 20) % (slack + 1)
    tallies = tallies.at[giver].add(-shifted).at[sink].add(shifted)
    labels = jnp.searchsorted(jnp.cumsum(tallies), jnp.arange(rows * top), side="right").astype(jnp.int32)
    table = labels.reshape(top, rows).T
    table = table[jax.random.permutation(jax.random.fold_in(own, 1), rows)]
    rotation = jax.random.randint(jax.random.fold_in(own, 2), (rows, 1), 0, top)
    return jnp.take_along_axis(table, (jnp.arange(top)[None, :] + rotation) % top, axis=1)


def load_shares(count, total, bound, skew, full):
    loads = [(1 << 20) // math.isqrt(rank ** skew) + 1 for rank in range(1, count + 1)]
    largest = bound if full else min(bound, max(-(-total // count), total * loads[0] // sum(loads)))
    least = 1 if total - largest >= count - 1 else 0
    counts, rest = [largest] + [least] * (count - 1), total - largest - least * (count - 1)
    while rest > 0:
        candidates = [i for i in range(1, count) if counts[i] < largest] or [i for i in range(1, count) if counts[i] < bound]
        whole, remaining = sum([loads[i] for i in candidates]), rest
        for i in candidates:
            extra = min(bound - counts[i], max(1, remaining * loads[i] // whole), rest)
            counts[i] = counts[i] + extra
            rest = rest - extra
    return np.array(counts)


def scatter_about(rng, extent, scale, bound, pieces=(), kind=jnp.bfloat16):
    values = scale * jax.random.normal(rng, extent, jnp.float32)
    if pieces:
        values = values * level_of(rng, extent, pieces, -0.22, 0.18)
    return jnp.clip(values, -bound, bound).astype(kind)


def setup_inputs(seed: int = 0) -> dict:
    splits = jax.random.split(jax.random.key(seed), 14)
    embeds = draw_embeds(jax.random.fold_in(splits[13], 71), 0)
    image_feats = scatter_about(splits[1], (IMGS, C_VIS), 1.0, 6.0, ((0, 8),))
    image_pos = draw_image_pos(jax.random.fold_in(splits[13], 71), 0)
    proj_w = scatter_about(splits[3], (C_VIS, D), C_VIS ** -0.5, 0.0625, ((0, 8), (1, 8)))
    proj_b = scatter_about(splits[4], (D,), 0.5, 3.0, ((0, 8),))
    norm_gain = jnp.clip(1.0 + 0.18 * jax.random.normal(splits[5], (D,), jnp.float32), 0.099609375, 1.8984375).astype(jnp.bfloat16)
    kv_w = scatter_about(splits[6], (D, KVH * 2 * HEAD), D ** -0.5, 0.0625, ((0, 8),))
    prompt_lengths = set_ends(jax.random.randint(splits[7], (PROMPTS,), PROMPT_LEN // 2, PROMPT_LEN + 1), jax.random.fold_in(splits[7], 1), PROMPT_LEN // 2, PROMPT_LEN).astype(jnp.int32)
    page_owner_keys = jax.random.split(jax.random.fold_in(splits[8], 1), PAGES // PAGES_DEV)
    page_owner_turns = jax.random.permutation(jax.random.fold_in(splits[8], 3), PAGES // PAGES_DEV)
    page_owner = jax.vmap(lambda own, number: assign_block(jax.random.fold_in(splits[8], 2), own, number, PAGES_DEV, N_SEQ, 1, CAP, 2))(page_owner_keys, page_owner_turns).reshape((PAGES, 1))
    queries = draw_queries(jax.random.fold_in(splits[13], 71), 0)
    kv_cache = draw_kv_cache(jax.random.fold_in(splits[13], 71), 0)
    new_kv = scatter_about(splits[11], (IMGS, KVH * 2 * HEAD), 1.0, 5.0, ((0, 8), (1, 8)))
    cache_lengths = set_ends(jax.random.randint(splits[12], (IMGS,), 2, CACHE + 1), jax.random.fold_in(splits[12], 1), 2, CACHE).astype(jnp.int32)
    return dict(embeds=embeds, image_feats=image_feats, image_pos=image_pos, proj_w=proj_w, proj_b=proj_b, norm_gain=norm_gain, kv_w=kv_w, prompt_lengths=prompt_lengths, page_owner=page_owner, queries=queries, kv_cache=kv_cache, new_kv=new_kv, cache_lengths=cache_lengths)


def reference(embeds, image_feats, image_pos, proj_w, proj_b, norm_gain, kv_w, prompt_lengths, page_owner, queries, kv_cache, new_kv, cache_lengths):
    projected = jnp.dot(image_feats, proj_w, preferred_element_type=jnp.float32) + proj_b.astype(jnp.float32)
    image_hidden = jax.nn.gelu(projected, approximate=False).astype(jnp.bfloat16)
    hidden = embeds.at[image_pos].set(image_hidden)
    hidden_f32 = hidden.astype(jnp.float32)
    squares = lax.optimization_barrier(jnp.sum(hidden_f32 * hidden_f32, axis=1))
    row_scale = lax.rsqrt(squares / D + 1e-05)
    scaled = (hidden_f32 * norm_gain.astype(jnp.float32)).astype(jnp.bfloat16)
    kv_full = jnp.dot(scaled, kv_w, preferred_element_type=jnp.float32) * row_scale[:, None]
    positions = jnp.arange(TOKENS, dtype=jnp.int32)
    prompt_limit = prompt_lengths[positions // PROMPT_LEN]
    is_live = positions % PROMPT_LEN < prompt_limit
    kv_rows = jnp.where(is_live[:, None], kv_full, 0.0).astype(jnp.bfloat16)
    kv_pages = kv_rows.reshape(N_SEQ, PAGES_DEV, PAGE, KVH * 2 * HEAD)
    owners = page_owner[:, 0].reshape(N_SEQ, PAGES_DEV)
    one_hot = (owners[:, :, None] == jnp.arange(N_SEQ, dtype=jnp.int32)[None, None, :]).astype(jnp.int32)
    page_rank = lax.optimization_barrier(jnp.sum((jnp.cumsum(one_hot, axis=1) - one_hot) * one_hot, axis=2))
    slot_index = owners * CAP + page_rank
    selector = (slot_index[:, None, :] == jnp.arange(N_SEQ * CAP, dtype=jnp.int32)[None, :, None]).astype(jnp.float32)
    by_owner = jnp.einsum('sdp,spte->sdte', selector, kv_pages.astype(jnp.float32), precision=lax.Precision.HIGHEST).astype(jnp.bfloat16)
    sent_view = by_owner.reshape(N_SEQ * N_SEQ * CAP, PAGE, KVH * 2 * HEAD)
    received_view = by_owner.reshape(N_SEQ, N_SEQ, CAP, PAGE, KVH * 2 * HEAD).transpose(1, 0, 2, 3, 4).reshape(N_SEQ * N_SEQ * CAP, PAGE, KVH * 2 * HEAD)
    page_slots = jnp.concatenate([sent_view, received_view], axis=0)
    row_count = queries.shape[0]
    grouped = queries.astype(jnp.float32).reshape(row_count, KVH, QH // KVH, HEAD)
    cache_f32 = kv_cache.astype(jnp.float32).reshape(row_count, CACHE, KVH, 2 * HEAD)
    fresh_kv = new_kv.astype(jnp.float32).reshape(row_count, KVH, 2 * HEAD)
    scores = jnp.einsum('rgqh,rjgh->rgqj', grouped, cache_f32[..., :HEAD], precision=lax.Precision.HIGHEST) * HEAD ** (-0.5)
    in_cache = jnp.arange(CACHE, dtype=jnp.int32)[None, :] < cache_lengths[:, None]
    scores = jnp.where(in_cache[:, None, None, :], scores, -1e+30)
    own_score = jnp.einsum('rgqh,rgh->rgq', grouped, fresh_kv[..., :HEAD], precision=lax.Precision.HIGHEST) * HEAD ** (-0.5)
    row_max = jnp.maximum(lax.optimization_barrier(jnp.max(scores, axis=3)), own_score)
    weights = jnp.exp(scores - row_max[..., None])
    own_weight = jnp.exp(own_score - row_max)
    denominator = lax.optimization_barrier(jnp.sum(weights, axis=3)) + own_weight
    probability = lax.optimization_barrier((weights / denominator[..., None]).astype(jnp.bfloat16)).astype(jnp.float32)
    own_prob = lax.optimization_barrier((own_weight / denominator).astype(jnp.bfloat16)).astype(jnp.float32)
    attended = jnp.einsum('rgqj,rjgh->rgqh', probability, cache_f32[..., HEAD:], precision=lax.Precision.HIGHEST)
    attended = attended + own_prob[..., None] * fresh_kv[:, :, None, HEAD:]
    attended = attended.astype(jnp.bfloat16).reshape(row_count, QH * HEAD)
    row_states = jnp.concatenate([image_hidden, attended], axis=0)
    return (page_slots, row_states)
```

```python
import functools

import jax
import jax.numpy as jnp
from jax import lax
from jax.experimental import pallas as pl
from jax.experimental.pallas import tpu as pltpu
from jax.sharding import PartitionSpec as P

D = 8192
HEAD = 128
PAGE = 16
PROMPT_LEN = 4096
CAP = 32
ROWS = 2048
EXT = 32
TALL = ROWS + EXT
PAGES = ROWS // PAGE
IMG = 64
IMG_TALL = IMG + 16
BF = jnp.bfloat16
F32 = jnp.float32
VMEM_LIMIT = 56 * 1024 * 1024


def split_pair(value):
    high = value.astype(BF)
    low = (value - high.astype(F32)).astype(BF)
    return high, low


def project_kernel(place, embeds_ref, gain_ref, *refs):
    weights, (send_ref, keep_ref, squares_ref) = refs[:8], refs[8:]
    step = pl.program_id(0)

    @pl.when(step < 8)
    def _():
        hidden = embeds_ref[...].astype(F32)
        scaled = (hidden * gain_ref[...].astype(F32)).astype(BF)
        squared = hidden * hidden
        lanes = squared[:, 0:128]
        for k in range(1, 8):
            lanes = lanes + squared[:, k * 128 : (k + 1) * 128]
        summed = jnp.sum(lanes.T, axis=0, keepdims=True)
        squares_ref[pl.ds(2 * step, 1), :] = summed[:, :128]
        squares_ref[pl.ds(2 * step + 1, 1), :] = summed[:, 128:]
        for pair in range(4):
            weight = jnp.concatenate([weights[2 * pair][...], weights[2 * pair + 1][...]], axis=1)
            product = jnp.dot(scaled, weight, preferred_element_type=F32).astype(BF)
            target = send_ref if pair < 2 else keep_ref
            target[2 * (pair % 2)] = product[:, :128]
            target[2 * (pair % 2) + 1] = product[:, 128:]

    @pl.when(step == 8)
    def _():
        high, low = split_pair(squares_ref[...])
        both = jnp.concatenate([high, low], axis=0)
        for j in range(4):
            send_ref[j, 0:EXT, :] = both
            keep_ref[j, 0:EXT, :] = both


def project_text(place, embeds, gain, kv_w):
    def column(r, j):
        def index(i, place):
            core = place[1] if r else 1 - place[1]
            head = 2 * lax.rem(place[2] + j, 4) + core
            return (0, 2 * head + place[0])

        return index

    specs = [
        pl.BlockSpec((256, 1024), lambda i, place: (jnp.minimum(i, 7), 0)),
        pl.BlockSpec((1, 1024), lambda i, place: (0, 0)),
    ] + [pl.BlockSpec((1024, 128), column(r, j)) for r in range(2) for j in range(4)]
    out = jax.ShapeDtypeStruct((4, TALL, 128), BF)
    return pl.pallas_call(
        project_kernel,
        grid_spec=pltpu.PrefetchScalarGridSpec(
            num_scalar_prefetch=1,
            grid=(9,),
            in_specs=specs,
            out_specs=[pl.BlockSpec((4, 256, 128), lambda i, place: (0, i, 0))] * 2,
            scratch_shapes=[pltpu.VMEM((16, 128), F32)],
        ),
        out_shape=[out, out],
        compiler_params=pltpu.CompilerParams(vmem_limit_bytes=VMEM_LIMIT),
        cost_estimate=pl.CostEstimate(
            flops=2 * ROWS * 1024 * 1024, bytes_accessed=12 << 20, transcendentals=0
        ),
        name="project_text",
    )(place, embeds, gain, *([kv_w] * 8))


def add_kernel(a_ref, b_ref, out_ref):
    out_ref[0:ROWS, :] = (a_ref[0, 0:ROWS, :].astype(F32) + b_ref[0, 0:ROWS, :].astype(F32)).astype(BF)
    total = jnp.zeros((16, 128), F32)
    for ref in (a_ref, b_ref):
        total = total + ref[0, ROWS : ROWS + 16, :].astype(F32) + ref[0, ROWS + 16 : TALL, :].astype(F32)
    high, low = split_pair(total)
    out_ref[ROWS : ROWS + 16, :] = high
    out_ref[ROWS + 16 : TALL, :] = low


def add_pair(keep, received, j):
    spec = pl.BlockSpec((1, TALL, 128), lambda i: (j, 0, 0))
    return pl.pallas_call(
        add_kernel,
        grid=(1,),
        in_specs=[spec, spec],
        out_specs=pl.BlockSpec((TALL, 128), lambda i: (0, 0)),
        out_shape=jax.ShapeDtypeStruct((TALL, 128), BF),
        compiler_params=pltpu.CompilerParams(vmem_limit_bytes=VMEM_LIMIT),
        cost_estimate=pl.CostEstimate(flops=TALL * 128, bytes_accessed=3 << 19, transcendentals=0),
        name="add_pair",
    )(keep, received)


def finish_kernel(slots, limit, a_ref, b_ref, c_ref, d_ref, rows_ref, slot_ref):
    refs = (a_ref, b_ref, c_ref, d_ref)
    slot_ref[...] = jnp.zeros_like(slot_ref)
    squares = jnp.zeros((16, 128), F32)
    for ref in refs:
        squares = squares + ref[ROWS : ROWS + 16, :].astype(F32) + ref[ROWS + 16 : TALL, :].astype(F32)
    scale = lax.rsqrt(squares / D + 1e-05)
    row_iota = lax.broadcasted_iota(jnp.int32, (128, 128), 0)
    for part in range(16):
        tile = jnp.broadcast_to(scale[part : part + 1, :], (128, 128)).T
        here = pl.ds(part * 128, 128)
        total = refs[0][here, :].astype(F32)
        for ref in refs[1:]:
            total = total + ref[here, :].astype(F32)
        live = row_iota + part * 128 < limit[0]
        rows = jnp.where(live, total * tile, 0.0).astype(BF)
        for p in range(8):
            page = rows[p * PAGE : (p + 1) * PAGE, :]
            rows_ref[part * 8 + p] = page
            slot_ref[0, slots[part * 8 + p]] = page


def finish_text(slots, limit, parts):
    spec = pl.BlockSpec((TALL, 128), lambda i, slots, limit: (0, 0))
    return pl.pallas_call(
        finish_kernel,
        grid_spec=pltpu.PrefetchScalarGridSpec(
            num_scalar_prefetch=2,
            grid=(1,),
            in_specs=[spec] * 4,
            out_specs=[
                pl.BlockSpec((PAGES, PAGE, 128), lambda i, slots, limit: (0, 0, 0)),
                pl.BlockSpec((1, 256, PAGE, 128), lambda i, slots, limit: (1, 0, 0, 0)),
            ],
        ),
        out_shape=[
            jax.ShapeDtypeStruct((PAGES, PAGE, 128), BF),
            jax.ShapeDtypeStruct((2, 256, PAGE, 128), BF),
        ],
        compiler_params=pltpu.CompilerParams(vmem_limit_bytes=VMEM_LIMIT),
        cost_estimate=pl.CostEstimate(flops=ROWS * 1024, bytes_accessed=4 << 20, transcendentals=0),
        name="finish_text",
    )(slots, limit, *parts)


def place_kernel(slots, rows_ref, slot_ref):
    slot_ref[...] = jnp.zeros_like(slot_ref)
    for p in range(PAGES):
        slot_ref[slots[p]] = rows_ref[p]


def place_pages(slots, rows):
    return pl.pallas_call(
        place_kernel,
        grid_spec=pltpu.PrefetchScalarGridSpec(
            num_scalar_prefetch=1,
            grid=(1,),
            in_specs=[pl.BlockSpec((PAGES, PAGE, 128), lambda i, slots: (0, 0, 0))],
            out_specs=pl.BlockSpec((256, PAGE, 128), lambda i, slots: (0, 0, 0)),
        ),
        out_shape=jax.ShapeDtypeStruct((256, PAGE, 128), BF),
        compiler_params=pltpu.CompilerParams(vmem_limit_bytes=VMEM_LIMIT),
        cost_estimate=pl.CostEstimate(flops=ROWS * 128, bytes_accessed=3 << 19, transcendentals=0),
        name="place_pages",
    )(slots, rows)


def merge_kernel(place, own_ref, other_ref, first_ref, second_ref, image_ref, out_ref):
    match = jnp.where(place[0] == 0, pl.program_id(0), place[3]).astype(F32)
    targets = []
    for half in range(2):
        owner = image_ref[half, 0, IMG : IMG + 1, 0:IMG].astype(F32)
        rank = image_ref[half, 0, IMG + 1 : IMG + 2, 0:IMG].astype(F32)
        offset = image_ref[half, 0, IMG + 2 : IMG + 3, 0:IMG].astype(F32)
        targets.append(jnp.where(owner == match, rank * PAGE + offset, -1.0))
    target = jnp.concatenate(targets, axis=1)
    data = jnp.concatenate([image_ref[0, 0, 0:IMG, :], image_ref[1, 0, 0:IMG, :]], axis=0)
    spots = lax.broadcasted_iota(jnp.int32, (CAP * PAGE, 2 * IMG), 0).astype(F32)
    chosen = (spots == target).astype(F32).astype(BF)
    image = jnp.dot(chosen, data, preferred_element_type=F32)
    taken = jnp.dot(chosen, jnp.ones((2 * IMG, 256), BF), preferred_element_type=F32)

    def write(left, right):
        text = jnp.concatenate([left.reshape(CAP * PAGE, 128), right.reshape(CAP * PAGE, 128)], axis=1)
        merged = jnp.where(taken > 0.5, image, text.astype(F32)).astype(BF)
        out_ref[...] = merged.reshape(CAP, PAGE, 256)

    @pl.when(place[0] == 0)
    def _():
        write(own_ref[0], other_ref[...])

    @pl.when(place[0] != 0)
    def _():
        write(first_ref[0], second_ref[0])


def merge_slots(place, own, other, arrived, image):
    def local(i, place):
        return jnp.where(place[0] == 0, i, 7)

    def remote(i, place):
        return jnp.where(place[0] == 0, 0, i)

    return pl.pallas_call(
        merge_kernel,
        grid_spec=pltpu.PrefetchScalarGridSpec(
            num_scalar_prefetch=1,
            grid=(8,),
            in_specs=[
                pl.BlockSpec((1, CAP, PAGE, 128), lambda i, place: (1, local(i, place), 0, 0)),
                pl.BlockSpec((CAP, PAGE, 128), lambda i, place: (local(i, place), 0, 0)),
                pl.BlockSpec((1, CAP, PAGE, 128), lambda i, place: (0, remote(i, place), 0, 0)),
                pl.BlockSpec((1, CAP, PAGE, 128), lambda i, place: (1, remote(i, place), 0, 0)),
                pl.BlockSpec(
                    (2, 1, IMG_TALL, 256),
                    lambda i, place: (0, jnp.where(place[0] == 0, place[3], i), 0, 0),
                ),
            ],
            out_specs=pl.BlockSpec((CAP, PAGE, 256), lambda i, place: (i, 0, 0)),
        ),
        out_shape=jax.ShapeDtypeStruct((256, PAGE, 256), BF),
        compiler_params=pltpu.CompilerParams(vmem_limit_bytes=VMEM_LIMIT),
        cost_estimate=pl.CostEstimate(
            flops=2 * 8 * 512 * 128 * 512, bytes_accessed=5 << 20, transcendentals=0
        ),
        name="merge_slots",
    )(place, own, other, arrived, arrived, image)


def attend(queries, kv_cache, new_kv, cache_lengths):
    row_count = queries.shape[0]
    heads_kv = kv_cache.shape[2] // (2 * HEAD)
    grouped = queries.reshape(row_count, heads_kv, queries.shape[1] // (HEAD * heads_kv), HEAD)
    stored = kv_cache.reshape(row_count, kv_cache.shape[1], heads_kv, 2 * HEAD)
    fresh_kv = new_kv.reshape(row_count, heads_kv, 2 * HEAD)
    scores = jnp.einsum(
        "rgqh,rjgh->rgqj", grouped, stored[..., :HEAD], preferred_element_type=jnp.float32
    ) * HEAD ** (-0.5)
    in_cache = jnp.arange(stored.shape[1], dtype=jnp.int32)[None, :] < cache_lengths[:, None]
    scores = jnp.where(in_cache[:, None, None, :], scores, -1e30)
    own_score = jnp.einsum(
        "rgqh,rgh->rgq", grouped, fresh_kv[..., :HEAD], preferred_element_type=jnp.float32
    ) * HEAD ** (-0.5)
    row_max = jnp.maximum(jnp.max(scores, axis=3), own_score)
    weights = jnp.exp(scores - row_max[..., None])
    own_weight = jnp.exp(own_score - row_max)
    denominator = jnp.sum(weights, axis=3) + own_weight
    probability = (weights / denominator[..., None]).astype(jnp.bfloat16)
    own_prob = lax.optimization_barrier((own_weight / denominator).astype(jnp.bfloat16)).astype(
        jnp.float32
    )
    attended = jnp.einsum(
        "rgqj,rjgh->rgqh", probability, stored[..., HEAD:], preferred_element_type=jnp.float32
    )
    attended = attended + own_prob[..., None] * fresh_kv[:, :, None, HEAD:].astype(jnp.float32)
    return attended.astype(jnp.bfloat16).reshape(row_count, queries.shape[1])


PARTNER = [(i, i ^ 1) for i in range(8)]


def shift(k):
    return [(i, (i + 2 * k) % 8) for i in range(8)]


def per_device(
    embeds,
    image_feats,
    image_pos,
    proj_w,
    proj_b,
    norm_gain,
    kv_w,
    prompt_lengths,
    page_owner,
    queries,
    kv_cache,
    new_kv,
    cache_lengths,
):
    group = lax.axis_index("group").astype(jnp.int32)
    seq = lax.axis_index("seq").astype(jnp.int32)
    mp = lax.axis_index("mp").astype(jnp.int32)
    core, x = mp % 2, mp // 2
    place = jnp.stack([group, core, x, seq])
    gain = norm_gain.reshape(1, -1)

    mine = lax.dynamic_slice(image_feats, (group * IMG + core * 32, 0), (32, image_feats.shape[1]))
    depth = proj_w.shape[0]
    blocks = mine.reshape(32, 8, depth).transpose(1, 0, 2)
    got = lax.all_to_all(blocks, "seq", 0, 0, tiled=True)
    swapped = lax.ppermute(got, "mp", PARTNER)
    low = jnp.where(core == 0, got, swapped)
    high = jnp.where(core == 0, swapped, got)
    feats = jnp.concatenate([low, high], axis=1).reshape(8 * IMG, depth)

    send, keep = project_text(place, embeds, gain, kv_w)
    received = lax.ppermute(send, "mp", PARTNER)
    parts = [None] * 4
    for j in (1, 2, 3):
        parts[j] = lax.ppermute(add_pair(keep, received, j), "mp", shift(j))
    parts[0] = add_pair(keep, received, 0)

    partial = jnp.dot(feats, proj_w, preferred_element_type=F32).astype(BF)
    pieces = lax.all_to_all(partial, "seq", 0, 0, tiled=True).reshape(8, IMG, -1)
    summed = jnp.sum(pieces.astype(F32), axis=0)
    image_hidden = jax.nn.gelu(summed + proj_b.astype(F32), approximate=False).astype(BF)

    owners = page_owner[:, 0]
    one_hot = (owners[:, None] == jnp.arange(8, dtype=jnp.int32)[None, :]).astype(jnp.int32)
    before = (
        jnp.arange(PAGES, dtype=jnp.int32)[None, :] < jnp.arange(PAGES, dtype=jnp.int32)[:, None]
    )
    page_rank = jnp.sum((before & (owners[:, None] == owners[None, :])).astype(jnp.int32), axis=1)
    slots = owners * CAP + page_rank
    prompt = seq // 2
    live = jnp.sum(jnp.where(jnp.arange(4, dtype=jnp.int32) == prompt, prompt_lengths, 0))
    limit = live - (seq % 2) * ROWS

    hidden = image_hidden.astype(F32)
    squares = jnp.sum(hidden * hidden, axis=1)
    scaled = (hidden * norm_gain.astype(F32)).astype(BF)
    image_kv = jnp.dot(scaled, kv_w, preferred_element_type=F32).astype(BF)
    image_kv = image_kv.reshape(IMG, 8, 256).transpose(1, 0, 2)
    square_high, square_low = split_pair(squares)
    extra = jnp.concatenate([square_high, square_low]).reshape(2, IMG)
    extra = jnp.pad(extra, ((0, 14), (0, 256 - IMG)))
    extra = jnp.broadcast_to(extra[None], (8, 16, 256))
    image_parts = lax.all_to_all(jnp.concatenate([image_kv, extra], axis=1), "mp", 0, 0, tiled=True)
    image_sum = jnp.sum(image_parts.astype(F32), axis=0)
    image_squares = image_sum[IMG, :IMG] + image_sum[IMG + 1, :IMG]
    image_scale = lax.rsqrt(image_squares / D + 1e-05)
    local_pos = lax.dynamic_slice(image_pos, (group * IMG,), (IMG,)) - seq * ROWS
    image_rows = jnp.where(
        (local_pos < limit)[:, None], image_sum[:IMG] * image_scale[:, None], 0.0
    ).astype(BF)
    at_page = (local_pos // PAGE)[:, None] == jnp.arange(PAGES, dtype=jnp.int32)[None, :]
    image_owner = jnp.sum(jnp.where(at_page, owners[None, :], 0), axis=1)
    image_rank = jnp.sum(jnp.where(at_page, page_rank[None, :], 0), axis=1)
    labels = jnp.stack([image_owner, image_rank, local_pos % PAGE]).astype(BF)
    labels = jnp.pad(labels, ((0, 13), (0, 256 - IMG)))
    image_block = jnp.concatenate([image_rows, labels], axis=0)
    image_all = lax.all_gather(image_block, ("group", "seq"), axis=0)
    image_all = image_all.reshape(2, 8, IMG_TALL, 256)

    rows, by_owner = finish_text(slots, limit.reshape(1), parts)
    other_rows = lax.ppermute(rows, "group", [(1, 0)])
    arrived = lax.all_to_all(
        by_owner.reshape(512, PAGE, 128), ("group", "seq"), split_axis=0, concat_axis=0, tiled=True
    ).reshape(2, 256, PAGE, 128)
    other = place_pages(slots, other_rows)
    page_slots = merge_slots(place, by_owner, other, arrived, image_all)

    other_hidden = lax.ppermute(image_hidden, "group", [(1, 0)])
    attended = lax.cond(
        group != 0,
        attend,
        lambda *unused: jnp.zeros(queries.shape, BF),
        queries,
        kv_cache,
        new_kv,
        cache_lengths,
    )
    row_states = jnp.where(
        group == 0, jnp.concatenate([image_hidden, other_hidden], axis=0), attended
    )
    return (page_slots, row_states)


def solution(mesh):
    in_specs = (
        P("seq", "mp"),
        P("seq", None),
        P("seq"),
        P("seq", "mp"),
        P("mp"),
        P("mp"),
        P("mp", None),
        P(),
        P("seq", None),
        P("seq", "mp"),
        P("seq", None, "mp"),
        P("seq", "mp"),
        P("seq"),
    )
    out_specs = (P(("group", "seq"), None, "mp"), P(("group", "seq"), "mp"))
    return jax.shard_map(
        per_device, mesh=mesh, in_specs=in_specs, out_specs=out_specs, check_vma=False
    )
```

```python
import functools

import jax
import jax.numpy as jnp
from jax import lax
from jax.experimental import pallas as pl
from jax.experimental.pallas import tpu as pltpu
from jax.sharding import PartitionSpec as P

D = 8192
HEAD = 128
PAGE = 16
PROMPT_LEN = 4096
CAP = 32
ROWS = 2048
EXT = 32
TALL = ROWS + EXT
PAGES = ROWS // PAGE
IMG = 64
IMG_TALL = IMG + 16
BF = jnp.bfloat16
F32 = jnp.float32
LIGHT = pl.CostEstimate(flops=1, bytes_accessed=1, transcendentals=0)
VMEM_LIMIT = 56 * 1024 * 1024


def split_pair(value):
    high = value.astype(BF)
    low = (value - high.astype(F32)).astype(BF)
    return high, low


def project_kernel(count, place, embeds_ref, gain_ref, *refs):
    weights, refs = refs[: 2 * count], refs[2 * count :]
    if count == 2:
        send_ref, keep_ref, both_ref, squares_ref = refs
    step = pl.program_id(0)

    @pl.when(step < 8)
    def _():
        hidden = embeds_ref[...].astype(F32)
        scaled = (hidden * gain_ref[...].astype(F32)).astype(BF)
        squared = hidden * hidden
        lanes = squared[:, 0:128]
        for k in range(1, 8):
            lanes = lanes + squared[:, k * 128 : (k + 1) * 128]
        summed = jnp.sum(lanes.T, axis=0, keepdims=True)
        squares_ref[pl.ds(2 * step, 1), :] = summed[:, :128]
        squares_ref[pl.ds(2 * step + 1, 1), :] = summed[:, 128:]
        for target, pair in ((send_ref, weights[:2]), (keep_ref, weights[2:])):
            weight = jnp.concatenate([pair[0][...], pair[1][...]], axis=1)
            product = jnp.dot(scaled, weight, preferred_element_type=F32).astype(BF)
            target[0] = product[:, :128]
            target[1] = product[:, 128:]

    @pl.when(step == 8)
    def _():
        high, low = split_pair(squares_ref[...])
        both = jnp.concatenate([high, low], axis=0)
        for j in range(count):
            send_ref[j, 0:EXT, :] = both
            keep_ref[j, 0:EXT, :] = both


def project_text(place, embeds, gain, kv_w, shifts):
    def column(r, j):
        def index(i, place):
            core = place[1] if r else 1 - place[1]
            head = 2 * lax.rem(place[2] + j, 4) + core
            return (0, 2 * head + place[0])

        return index

    count = len(shifts)
    specs = [
        pl.BlockSpec((256, 1024), lambda i, place: (jnp.minimum(i, 7), 0)),
        pl.BlockSpec((1, 1024), lambda i, place: (0, 0)),
    ] + [pl.BlockSpec((1024, 128), column(r, j)) for r in range(2) for j in shifts]
    out = jax.ShapeDtypeStruct((count, TALL, 128), BF)
    return pl.pallas_call(
        functools.partial(project_kernel, count),
        grid_spec=pltpu.PrefetchScalarGridSpec(
            num_scalar_prefetch=1,
            grid=(9,),
            in_specs=specs,
            out_specs=[pl.BlockSpec((count, 256, 128), lambda i, place: (0, i, 0))] * 2
            + [pl.BlockSpec((8, 128), lambda i, place: (0, 0))],
            scratch_shapes=[pltpu.VMEM((16, 128), F32)],
        ),
        out_shape=[out, out, jax.ShapeDtypeStruct((8, 128), F32)],
        compiler_params=pltpu.CompilerParams(vmem_limit_bytes=VMEM_LIMIT),
        cost_estimate=LIGHT,
        name="project_text",
    )(place, embeds, gain, *([kv_w] * (2 * count)))


def add_kernel(a_ref, b_ref, out_ref):
    out_ref[...] = (a_ref[0].astype(F32) + b_ref[0].astype(F32)).astype(BF)

    @pl.when(pl.program_id(0) == 1)
    def _():
        half = TALL // 2
        total = jnp.zeros((16, 128), F32)
        for ref in (a_ref, b_ref):
            total = total + ref[0, half - 32 : half - 16, :].astype(F32) + ref[0, half - 16 :, :].astype(F32)
        high, low = split_pair(total)
        out_ref[half - 32 : half - 16, :] = high
        out_ref[half - 16 :, :] = low


def add_pair(keep, received, j):
    spec = pl.BlockSpec((1, TALL // 2, 128), lambda i: (j, i, 0))
    return pl.pallas_call(
        add_kernel,
        grid=(2,),
        in_specs=[spec, spec],
        out_specs=pl.BlockSpec((TALL // 2, 128), lambda i: (i, 0)),
        out_shape=jax.ShapeDtypeStruct((TALL, 128), BF),
        compiler_params=pltpu.CompilerParams(vmem_limit_bytes=VMEM_LIMIT),
        cost_estimate=LIGHT,
        name="add_pair",
    )(keep, received)


def finish_kernel(slots, limit, a_ref, b_ref, c_ref, d_ref, rows_ref, slot_ref):
    refs = (a_ref, b_ref, c_ref, d_ref)
    slot_ref[...] = jnp.zeros_like(slot_ref)
    squares = jnp.zeros((16, 128), F32)
    for ref in refs:
        squares = squares + ref[ROWS : ROWS + 16, :].astype(F32) + ref[ROWS + 16 : TALL, :].astype(F32)
    scale = lax.rsqrt(squares / D + 1e-05)
    row_iota = lax.broadcasted_iota(jnp.int32, (128, 128), 0)
    for part in range(16):
        tile = jnp.broadcast_to(scale[part : part + 1, :], (128, 128)).T
        here = pl.ds(part * 128, 128)
        total = refs[0][here, :].astype(F32)
        for ref in refs[1:]:
            total = total + ref[here, :].astype(F32)
        live = row_iota + part * 128 < limit[0]
        rows = jnp.where(live, total * tile, 0.0).astype(BF)
        for p in range(8):
            page = rows[p * PAGE : (p + 1) * PAGE, :]
            rows_ref[part * 8 + p] = page
            slot_ref[0, slots[part * 8 + p]] = page


def finish_text(slots, limit, parts):
    spec = pl.BlockSpec((TALL, 128), lambda i, slots, limit: (0, 0))
    return pl.pallas_call(
        finish_kernel,
        grid_spec=pltpu.PrefetchScalarGridSpec(
            num_scalar_prefetch=2,
            grid=(1,),
            in_specs=[spec] * 4,
            out_specs=[
                pl.BlockSpec((PAGES, PAGE, 128), lambda i, slots, limit: (0, 0, 0)),
                pl.BlockSpec((1, 256, PAGE, 128), lambda i, slots, limit: (1, 0, 0, 0)),
            ],
        ),
        out_shape=[
            jax.ShapeDtypeStruct((PAGES, PAGE, 128), BF),
            jax.ShapeDtypeStruct((2, 256, PAGE, 128), BF),
        ],
        compiler_params=pltpu.CompilerParams(vmem_limit_bytes=VMEM_LIMIT),
        cost_estimate=LIGHT,
        name="finish_text",
    )(slots, limit, *parts)


def place_kernel(slots, rows_ref, slot_ref):
    slot_ref[...] = jnp.zeros_like(slot_ref)
    for p in range(PAGES):
        slot_ref[slots[p]] = rows_ref[p]


def place_pages(slots, rows):
    return pl.pallas_call(
        place_kernel,
        grid_spec=pltpu.PrefetchScalarGridSpec(
            num_scalar_prefetch=1,
            grid=(1,),
            in_specs=[pl.BlockSpec((PAGES, PAGE, 128), lambda i, slots: (0, 0, 0))],
            out_specs=pl.BlockSpec((256, PAGE, 128), lambda i, slots: (0, 0, 0)),
        ),
        out_shape=jax.ShapeDtypeStruct((256, PAGE, 128), BF),
        compiler_params=pltpu.CompilerParams(vmem_limit_bytes=VMEM_LIMIT),
        cost_estimate=LIGHT,
        name="place_pages",
    )(slots, rows)


def cut_kernel(place, feats_ref, out_ref):
    depth = out_ref.shape[2]
    for k in range(8):
        out_ref[k] = feats_ref[:, k * depth : (k + 1) * depth]


def cut_features(place, feats):
    depth = feats.shape[1] // 8
    return pl.pallas_call(
        cut_kernel,
        grid_spec=pltpu.PrefetchScalarGridSpec(
            num_scalar_prefetch=1,
            grid=(1,),
            in_specs=[
                pl.BlockSpec((32, feats.shape[1]), lambda i, place: (2 * place[0] + place[1], 0))
            ],
            out_specs=pl.BlockSpec((8, 32, depth), lambda i, place: (0, 0, 0)),
        ),
        out_shape=jax.ShapeDtypeStruct((8, 32, depth), BF),
        cost_estimate=LIGHT,
        name="cut_features",
    )(place, feats)


def partial_kernel(place, got_ref, swapped_ref, weight_ref, out_ref):
    def product(ref):
        rows = ref[...].reshape(256, ref.shape[2])
        value = jnp.dot(rows, weight_ref[...], preferred_element_type=F32).astype(BF)
        out_ref[...] = value.reshape(8, 32, value.shape[1])

    own = pl.program_id(0) == place[1]

    @pl.when(own)
    def _():
        product(got_ref)

    @pl.when(jnp.logical_not(own))
    def _():
        product(swapped_ref)


def partial_images(place, got, swapped, weight):
    depth, width = weight.shape
    rows = pl.BlockSpec((8, 32, depth), lambda i, place: (0, 0, 0))
    return pl.pallas_call(
        partial_kernel,
        grid_spec=pltpu.PrefetchScalarGridSpec(
            num_scalar_prefetch=1,
            grid=(2,),
            in_specs=[rows, rows, pl.BlockSpec((depth, width), lambda i, place: (0, 0))],
            out_specs=pl.BlockSpec((8, 32, width), lambda i, place: (0, i, 0)),
        ),
        out_shape=jax.ShapeDtypeStruct((8, IMG, width), BF),
        compiler_params=pltpu.CompilerParams(vmem_limit_bytes=VMEM_LIMIT),
        cost_estimate=LIGHT,
        name="partial_images",
    )(place, got, swapped, weight)


def image_kernel(
    place, pieces_ref, bias_ref, gain_ref, weight_ref, hidden_ref, swap_ref, same_ref, scaled, pair
):
    step = pl.program_id(0)

    @pl.when(step == 0)
    def _():
        total = pieces_ref[0].astype(F32)
        for k in range(1, 8):
            total = total + pieces_ref[k].astype(F32)
        total = total + bias_ref[...].astype(F32)
        image_hidden = (0.5 * total * (1.0 + lax.erf(total * (0.5**0.5)))).astype(BF)
        hidden_ref[...] = image_hidden
        hidden = image_hidden.astype(F32)
        scaled[...] = (hidden * gain_ref[...].astype(F32)).astype(BF)
        squared = hidden * hidden
        lanes = squared[:, 0:128]
        for k in range(1, 8):
            lanes = lanes + squared[:, k * 128 : (k + 1) * 128]
        lanes = jnp.concatenate([lanes, jnp.zeros_like(lanes)], axis=0)
        summed = jnp.sum(lanes.T, axis=0, keepdims=True)
        high, low = split_pair(summed)
        picked = lax.broadcasted_iota(jnp.int32, (16, 128), 0)
        rows = jnp.where(picked == 0, high.astype(F32), jnp.where(picked == 1, low.astype(F32), 0.0))
        pair[...] = jnp.concatenate([rows, jnp.zeros_like(rows)], axis=1).astype(BF)

    product = jnp.dot(scaled[...], weight_ref[...], preferred_element_type=F32).astype(BF)
    block = jnp.concatenate([product, pair[...]], axis=0)

    @pl.when(step < 4)
    def _():
        swap_ref[0] = block

    @pl.when(step >= 4)
    def _():
        same_ref[0] = block


def image_rows_kv(place, pieces, bias, gain, kv_w):
    def column(i, place):
        core = jnp.where(i < 4, 1 - place[1], place[1])
        return (0, 2 * lax.rem(place[2] + i, 4) + core)

    width = pieces.shape[2]
    row = pl.BlockSpec((1, width), lambda i, place: (0, 0))
    out = jax.ShapeDtypeStruct((4, IMG_TALL, 256), BF)
    return pl.pallas_call(
        image_kernel,
        grid_spec=pltpu.PrefetchScalarGridSpec(
            num_scalar_prefetch=1,
            grid=(8,),
            in_specs=[
                pl.BlockSpec((8, IMG, width), lambda i, place: (0, 0, 0)),
                row,
                row,
                pl.BlockSpec((width, 256), column),
            ],
            out_specs=[
                pl.BlockSpec((IMG, width), lambda i, place: (0, 0)),
                pl.BlockSpec((1, IMG_TALL, 256), lambda i, place: (jnp.minimum(i, 3), 0, 0)),
                pl.BlockSpec((1, IMG_TALL, 256), lambda i, place: (jnp.maximum(i - 4, 0), 0, 0)),
            ],
            scratch_shapes=[pltpu.VMEM((IMG, width), BF), pltpu.VMEM((16, 256), BF)],
        ),
        out_shape=[jax.ShapeDtypeStruct((IMG, width), BF), out, out],
        compiler_params=pltpu.CompilerParams(vmem_limit_bytes=VMEM_LIMIT),
        cost_estimate=LIGHT,
        name="image_rows_kv",
    )(place, pieces, bias, gain, kv_w)


def pair_kernel(same_ref, received_ref, *out_refs):
    for j, out_ref in enumerate(out_refs):
        total = same_ref[j].astype(F32) + received_ref[j].astype(F32)
        out_ref[0:IMG, :] = total[0:IMG].astype(BF)
        high, low = split_pair(total[IMG : IMG + 1] + total[IMG + 1 : IMG + 2])
        picked = lax.broadcasted_iota(jnp.int32, (16, 256), 0)
        rows = jnp.where(picked == 0, high.astype(F32), jnp.where(picked == 1, low.astype(F32), 0.0))
        out_ref[IMG:, :] = rows.astype(BF)


def pair_images(same, received):
    return pl.pallas_call(
        pair_kernel,
        out_shape=[jax.ShapeDtypeStruct((IMG_TALL, 256), BF)] * 4,
        cost_estimate=LIGHT,
        name="pair_images",
    )(same, received)


def close_kernel(a_ref, b_ref, c_ref, d_ref, labels_ref, out_ref):
    total = a_ref[...].astype(F32) + b_ref[...].astype(F32)
    total = total + c_ref[...].astype(F32) + d_ref[...].astype(F32)
    squares = total[IMG : IMG + 1, 0:128] + total[IMG + 1 : IMG + 2, 0:128]
    scale = lax.rsqrt(squares / D + 1e-05)
    scale = jnp.where(labels_ref[3:4, 0:128].astype(F32) > 0.5, scale, 0.0)
    tile = jnp.broadcast_to(scale, (128, 128)).T[0:IMG]
    tile = jnp.concatenate([tile, tile], axis=1)
    out_ref[0:IMG, :] = jnp.where(tile > 0.0, total[0:IMG] * tile, 0.0).astype(BF)
    out_ref[IMG:, :] = labels_ref[...]


def close_images(parts, labels):
    return pl.pallas_call(
        close_kernel,
        out_shape=jax.ShapeDtypeStruct((IMG_TALL, 256), BF),
        cost_estimate=LIGHT,
        name="close_images",
    )(*parts, labels)


def merge_kernel(
    place, own_ref, other_ref, first_ref, second_ref, near_ref, yonder_ref, side_ref, far_ref, out_ref
):
    step = pl.program_id(0)
    match = jnp.where(place[0] == 0, step, place[3]).astype(F32)
    shard = jnp.where(place[0] == 0, place[3], step)
    level = lax.rem(place[3] - shard + 8, 4)
    close = (shard >= 4) == (place[3] >= 4)
    images = []
    for near, away in ((near_ref, yonder_ref), (side_ref, far_ref)):
        images.append(jnp.where(close, near[level].astype(F32), away[level].astype(F32)))
    targets = []
    for image in images:
        owner = image[IMG : IMG + 1, 0:IMG]
        spot = image[IMG + 1 : IMG + 2, 0:IMG] * PAGE + image[IMG + 2 : IMG + 3, 0:IMG]
        targets.append(jnp.where(owner == match, spot, -1.0))
    target = jnp.concatenate(targets, axis=1)
    data = jnp.concatenate([images[0][0:IMG], images[1][0:IMG]], axis=0).astype(BF)
    spots = lax.broadcasted_iota(jnp.int32, (CAP * PAGE, 2 * IMG), 0).astype(F32)
    chosen = (spots == target).astype(F32).astype(BF)
    image = jnp.dot(chosen, data, preferred_element_type=F32)
    taken = jnp.dot(chosen, jnp.ones((2 * IMG, 256), BF), preferred_element_type=F32)

    def write(left, right):
        text = jnp.concatenate([left.reshape(CAP * PAGE, 128), right.reshape(CAP * PAGE, 128)], axis=1)
        merged = jnp.where(taken > 0.5, image, text.astype(F32)).astype(BF)
        out_ref[...] = merged.reshape(CAP, PAGE, 256)

    @pl.when(place[0] == 0)
    def _():
        write(own_ref[0], other_ref[...])

    @pl.when(place[0] != 0)
    def _():
        write(first_ref[0], second_ref[0])


def merge_slots(place, own, other, arrived, images):
    def local(i, place):
        return jnp.where(place[0] == 0, i, 7)

    def remote(i, place):
        return jnp.where(place[0] == 0, 0, i)

    image_spec = pl.BlockSpec((4, IMG_TALL, 256), lambda i, place: (0, 0, 0))
    return pl.pallas_call(
        merge_kernel,
        grid_spec=pltpu.PrefetchScalarGridSpec(
            num_scalar_prefetch=1,
            grid=(8,),
            in_specs=[
                pl.BlockSpec((1, CAP, PAGE, 128), lambda i, place: (1, local(i, place), 0, 0)),
                pl.BlockSpec((CAP, PAGE, 128), lambda i, place: (local(i, place), 0, 0)),
                pl.BlockSpec((1, CAP, PAGE, 128), lambda i, place: (0, remote(i, place), 0, 0)),
                pl.BlockSpec((1, CAP, PAGE, 128), lambda i, place: (1, remote(i, place), 0, 0)),
            ]
            + [image_spec] * 4,
            out_specs=pl.BlockSpec((CAP, PAGE, 256), lambda i, place: (i, 0, 0)),
        ),
        out_shape=jax.ShapeDtypeStruct((256, PAGE, 256), BF),
        compiler_params=pltpu.CompilerParams(vmem_limit_bytes=VMEM_LIMIT),
        cost_estimate=LIGHT,
        name="merge_slots",
    )(place, own, other, arrived, arrived, *images)


def attend(queries, kv_cache, new_kv, cache_lengths):
    row_count = queries.shape[0]
    heads_kv = kv_cache.shape[2] // (2 * HEAD)
    grouped = queries.reshape(row_count, heads_kv, queries.shape[1] // (HEAD * heads_kv), HEAD)
    stored = kv_cache.reshape(row_count, kv_cache.shape[1], heads_kv, 2 * HEAD)
    fresh_kv = new_kv.reshape(row_count, heads_kv, 2 * HEAD)
    scores = jnp.einsum(
        "rgqh,rjgh->rgqj", grouped, stored[..., :HEAD], preferred_element_type=jnp.float32
    ) * HEAD ** (-0.5)
    in_cache = jnp.arange(stored.shape[1], dtype=jnp.int32)[None, :] < cache_lengths[:, None]
    scores = jnp.where(in_cache[:, None, None, :], scores, -1e30)
    own_score = jnp.einsum(
        "rgqh,rgh->rgq", grouped, fresh_kv[..., :HEAD], preferred_element_type=jnp.float32
    ) * HEAD ** (-0.5)
    row_max = jnp.maximum(jnp.max(scores, axis=3), own_score)
    weights = jnp.exp(scores - row_max[..., None])
    own_weight = jnp.exp(own_score - row_max)
    denominator = jnp.sum(weights, axis=3) + own_weight
    probability = (weights / denominator[..., None]).astype(jnp.bfloat16)
    own_prob = lax.optimization_barrier((own_weight / denominator).astype(jnp.bfloat16)).astype(
        jnp.float32
    )
    attended = jnp.einsum(
        "rgqj,rjgh->rgqh", probability, stored[..., HEAD:], preferred_element_type=jnp.float32
    )
    attended = attended + own_prob[..., None] * fresh_kv[:, :, None, HEAD:].astype(jnp.float32)
    return attended.astype(jnp.bfloat16).reshape(row_count, queries.shape[1])


PARTNER = [(i, i ^ 1) for i in range(8)]


def shift(k):
    return [(i, (i + 2 * k) % 8) for i in range(8)]


def seq_shift(y, z):
    return [(i, (i // 4 + y) % 2 * 4 + (i + z) % 4) for i in range(8)]


FAR = [(g * 8 + i, (1 - g) * 8 + (i + 4) % 8) for g in range(2) for i in range(8)]


def after(value, other):
    return lax.optimization_barrier((value, other))[0]


def per_device(
    embeds,
    image_feats,
    image_pos,
    proj_w,
    proj_b,
    norm_gain,
    kv_w,
    prompt_lengths,
    page_owner,
    queries,
    kv_cache,
    new_kv,
    cache_lengths,
):
    group = lax.axis_index("group").astype(jnp.int32)
    seq = lax.axis_index("seq").astype(jnp.int32)
    mp = lax.axis_index("mp").astype(jnp.int32)
    core, x = mp % 2, mp // 2
    place = jnp.stack([group, core, x, seq])
    gain = norm_gain.reshape(1, -1)

    bias = proj_b.reshape(1, -1)

    owners = page_owner[:, 0]
    before = (
        jnp.arange(PAGES, dtype=jnp.int32)[None, :] < jnp.arange(PAGES, dtype=jnp.int32)[:, None]
    )
    page_rank = jnp.sum((before & (owners[:, None] == owners[None, :])).astype(jnp.int32), axis=1)
    slots = owners * CAP + page_rank
    live = jnp.sum(jnp.where(jnp.arange(4, dtype=jnp.int32) == seq // 2, prompt_lengths, 0))
    limit = live - (seq % 2) * ROWS
    local_pos = lax.dynamic_slice(image_pos, (group * IMG,), (IMG,)) - seq * ROWS
    at_page = (local_pos // PAGE)[:, None] == jnp.arange(PAGES, dtype=jnp.int32)[None, :]
    image_owner = jnp.sum(jnp.where(at_page, owners[None, :], 0), axis=1)
    image_rank = jnp.sum(jnp.where(at_page, page_rank[None, :], 0), axis=1)
    labels = jnp.stack(
        [image_owner, image_rank, local_pos % PAGE, (local_pos < limit).astype(jnp.int32)]
    ).astype(BF)
    labels = jnp.pad(labels, ((0, 12), (0, 256 - IMG)))

    got = lax.all_to_all(cut_features(place, image_feats), "seq", 0, 0, tiled=True)

    send, keep, _ = project_text(place, embeds, gain, kv_w, (1, 3))
    received = lax.ppermute(send, "mp", PARTNER)
    got = after(got, keep)
    swapped = lax.ppermute(got, "mp", PARTNER)
    added = [None] * 4
    parts = [None] * 4
    for k, j in enumerate((1, 3)):
        added[j] = add_pair(keep, received, k)
        parts[j] = lax.ppermute(added[j], "mp", shift(j))
    send, keep, _ = project_text(place, after(embeds, (added[1], added[3])), gain, kv_w, (2, 0))
    received = lax.ppermute(send, "mp", PARTNER)
    for k, j in enumerate((2, 0)):
        added[j] = add_pair(keep, received, k)
    parts[2] = lax.ppermute(added[2], "mp", shift(2))
    parts[0] = added[0]

    swapped = after(swapped, (added[2], added[0]))
    partial = partial_images(place, got, swapped, proj_w)
    attended = lax.cond(
        group != 0,
        attend,
        lambda *unused: jnp.zeros(queries.shape, BF),
        after(queries, partial),
        kv_cache,
        new_kv,
        cache_lengths,
    )
    pieces = lax.all_to_all(partial, "seq", 0, 0, tiled=True)
    pieces = after(pieces, attended)
    image_hidden, swap, same = image_rows_kv(place, pieces, bias, gain, kv_w)
    image_pairs = pair_images(same, lax.ppermute(swap, "mp", PARTNER))
    image_parts = [image_pairs[0]]
    image_parts += [lax.ppermute(image_pairs[j], "mp", shift(j)) for j in (1, 2, 3)]

    rows, by_owner = finish_text(slots, limit.reshape(1), parts)
    other_rows = lax.ppermute(rows, "group", [(1, 0)])
    arrived = lax.all_to_all(
        by_owner.reshape(512, PAGE, 128), ("group", "seq"), split_axis=0, concat_axis=0, tiled=True
    ).reshape(2, 256, PAGE, 128)

    image_parts = after(image_parts, by_owner)
    image_block = close_images(image_parts, labels)
    near = jnp.stack(
        [image_block] + [lax.ppermute(image_block, "seq", seq_shift(0, k)) for k in (1, 2, 3)]
    )
    images = [
        near,
        lax.ppermute(near, "seq", seq_shift(1, 0)),
        lax.ppermute(near, "group", [(0, 1), (1, 0)]),
        lax.ppermute(near, ("group", "seq"), FAR),
    ]
    other = place_pages(slots, other_rows)
    page_slots = merge_slots(place, by_owner, other, arrived, images)

    other_hidden = lax.ppermute(image_hidden, "group", [(1, 0)])
    row_states = jnp.where(
        group == 0, jnp.concatenate([image_hidden, other_hidden], axis=0), attended
    )
    return (page_slots, row_states)


def solution(mesh):
    in_specs = (
        P("seq", "mp"),
        P("seq", None),
        P("seq"),
        P("seq", "mp"),
        P("mp"),
        P("mp"),
        P("mp", None),
        P(),
        P("seq", None),
        P("seq", "mp"),
        P("seq", None, "mp"),
        P("seq", "mp"),
        P("seq"),
    )
    out_specs = (P(("group", "seq"), None, "mp"), P(("group", "seq"), "mp"))
    return jax.shard_map(
        per_device, mesh=mesh, in_specs=in_specs, out_specs=out_specs, check_vma=False
    )
```

```python
import functools

import jax
import jax.numpy as jnp
from jax import lax
from jax.experimental import pallas as pl
from jax.experimental.pallas import tpu as pltpu
from jax.sharding import PartitionSpec as P

D = 8192
HEAD = 128
PAGE = 16
PROMPT_LEN = 4096
CAP = 32
ROWS = 2048
EXT = 32
TALL = ROWS + EXT
PAGES = ROWS // PAGE
IMG = 64
IMG_TALL = IMG + 16
BF = jnp.bfloat16
F32 = jnp.float32
def work(micros):
    size = int(micros * 3700000)
    return pl.CostEstimate(flops=micros * 1000000, bytes_accessed=size, transcendentals=0)


LIGHT = pl.CostEstimate(flops=1, bytes_accessed=1, transcendentals=0)
VMEM_LIMIT = 56 * 1024 * 1024


def split_pair(value):
    high = value.astype(BF)
    low = (value - high.astype(F32)).astype(BF)
    return high, low


TILE = 512
STEPS = ROWS // TILE


def project_kernel(place, embeds_ref, gain_ref, *refs):
    weights, send, keep, squares_ref = refs[0:8], refs[8:12], refs[12:16], refs[16]
    step = pl.program_id(0)

    @pl.when(step < STEPS)
    def _():
        hidden = embeds_ref[...].astype(F32)
        scaled = (hidden * gain_ref[...].astype(F32)).astype(BF)
        squared = hidden * hidden
        lanes = squared[:, 0:128]
        for k in range(1, 8):
            lanes = lanes + squared[:, k * 128 : (k + 1) * 128]
        summed = jnp.sum(lanes.T, axis=0, keepdims=True)
        for k in range(TILE // 128):
            squares_ref[pl.ds(TILE // 128 * step + k, 1), :] = summed[:, k * 128 : (k + 1) * 128]
        for k, target in enumerate((send[:2], send[2:], keep[:2], keep[2:])):
            weight = jnp.concatenate([weights[2 * k][...], weights[2 * k + 1][...]], axis=1)
            product = jnp.dot(scaled, weight, preferred_element_type=F32).astype(BF)
            target[0][...] = product[:, :128]
            target[1][...] = product[:, 128:]

    @pl.when(step == STEPS)
    def _():
        high, low = split_pair(squares_ref[...])
        both = jnp.concatenate([high, low], axis=0)
        for ref in (*send, *keep):
            ref[0:EXT, :] = both


def project_text(place, embeds, gain, kv_w):
    def column(r, j):
        def index(i, place):
            core = place[1] if r else 1 - place[1]
            head = 2 * lax.rem(place[2] + j, 4) + core
            return (0, 2 * head + place[0])

        return index

    specs = [
        pl.BlockSpec((TILE, 1024), lambda i, place: (jnp.minimum(i, STEPS - 1), 0)),
        pl.BlockSpec((1, 1024), lambda i, place: (0, 0)),
    ] + [pl.BlockSpec((1024, 128), column(r, j)) for r in range(2) for j in range(4)]
    outs = pl.pallas_call(
        project_kernel,
        grid_spec=pltpu.PrefetchScalarGridSpec(
            num_scalar_prefetch=1,
            grid=(STEPS + 1,),
            in_specs=specs,
            out_specs=[pl.BlockSpec((TILE, 128), lambda i, place: (i, 0))] * 8,
            scratch_shapes=[pltpu.VMEM((16, 128), F32)],
        ),
        out_shape=[jax.ShapeDtypeStruct((TALL, 128), BF)] * 8,
        compiler_params=pltpu.CompilerParams(vmem_limit_bytes=VMEM_LIMIT),
        cost_estimate=LIGHT,
        name="project_text",
    )(place, embeds, gain, *([kv_w] * 8))
    return outs[:4], outs[4:]


def square_rows(refs):
    total = jnp.zeros((16, 128), F32)
    for ref in refs:
        total = total + ref[ROWS : ROWS + 16, :].astype(F32) + ref[ROWS + 16 : TALL, :].astype(F32)
    return total


def add_kernel(a_ref, b_ref, out_ref):
    out_ref[0:ROWS, :] = (a_ref[0:ROWS, :].astype(F32) + b_ref[0:ROWS, :].astype(F32)).astype(BF)
    high, low = split_pair(square_rows([a_ref, b_ref]))
    out_ref[ROWS : ROWS + 16, :] = high
    out_ref[ROWS + 16 : TALL, :] = low


def add_pair(keep, received):
    return pl.pallas_call(
        add_kernel,
        out_shape=jax.ShapeDtypeStruct((TALL, 128), BF),
        compiler_params=pltpu.CompilerParams(vmem_limit_bytes=VMEM_LIMIT),
        cost_estimate=LIGHT,
        name="add_pair",
    )(keep, received)


def finish_kernel(slots, limit, *refs):
    parts, (rows_ref, slot_ref) = refs[:5], refs[5:]
    slot_ref[...] = jnp.zeros_like(slot_ref)
    squares = square_rows(parts)
    scale = lax.rsqrt(squares / D + 1e-05)
    row_iota = lax.broadcasted_iota(jnp.int32, (128, 128), 0)
    for part in range(16):
        tile = jnp.broadcast_to(scale[part : part + 1, :], (128, 128)).T
        here = slice(part * 128, part * 128 + 128)
        total = parts[0][here, :].astype(F32)
        for ref in parts[1:]:
            total = total + ref[here, :].astype(F32)
        live = row_iota + part * 128 < limit[0]
        rows = jnp.where(live, total * tile, 0.0).astype(BF)
        for p in range(8):
            page = rows[p * PAGE : (p + 1) * PAGE, :]
            rows_ref[part * 8 + p] = page
            slot_ref[0, slots[part * 8 + p]] = page


def finish_text(slots, limit, parts):
    whole = lambda i, slots, limit: (0, 0)
    return pl.pallas_call(
        finish_kernel,
        grid_spec=pltpu.PrefetchScalarGridSpec(
            num_scalar_prefetch=2,
            grid=(1,),
            in_specs=[pl.BlockSpec((TALL, 128), whole)] * 5,
            out_specs=[
                pl.BlockSpec((PAGES, PAGE, 128), lambda i, slots, limit: (0, 0, 0)),
                pl.BlockSpec((1, 256, PAGE, 128), lambda i, slots, limit: (1, 0, 0, 0)),
            ],
        ),
        out_shape=[
            jax.ShapeDtypeStruct((PAGES, PAGE, 128), BF),
            jax.ShapeDtypeStruct((2, 256, PAGE, 128), BF),
        ],
        compiler_params=pltpu.CompilerParams(vmem_limit_bytes=VMEM_LIMIT),
        cost_estimate=work(200000),
        name="finish_text",
    )(slots, limit, *parts)


def place_kernel(slots, rows_ref, slot_ref):
    slot_ref[...] = jnp.zeros_like(slot_ref)
    for p in range(PAGES):
        slot_ref[slots[p]] = rows_ref[p]


def place_pages(slots, rows):
    return pl.pallas_call(
        place_kernel,
        grid_spec=pltpu.PrefetchScalarGridSpec(
            num_scalar_prefetch=1,
            grid=(1,),
            in_specs=[pl.BlockSpec((PAGES, PAGE, 128), lambda i, slots: (0, 0, 0))],
            out_specs=pl.BlockSpec((256, PAGE, 128), lambda i, slots: (0, 0, 0)),
        ),
        out_shape=jax.ShapeDtypeStruct((256, PAGE, 128), BF),
        compiler_params=pltpu.CompilerParams(vmem_limit_bytes=VMEM_LIMIT),
        cost_estimate=LIGHT,
        name="place_pages",
    )(slots, rows)


def cut_kernel(place, feats_ref, out_ref):
    depth = out_ref.shape[2]
    for k in range(8):
        out_ref[k] = feats_ref[:, k * depth : (k + 1) * depth]


def cut_features(place, feats):
    depth = feats.shape[1] // 8
    return pl.pallas_call(
        cut_kernel,
        grid_spec=pltpu.PrefetchScalarGridSpec(
            num_scalar_prefetch=1,
            grid=(1,),
            in_specs=[
                pl.BlockSpec((32, feats.shape[1]), lambda i, place: (2 * place[0] + place[1], 0))
            ],
            out_specs=pl.BlockSpec((8, 32, depth), lambda i, place: (0, 0, 0)),
        ),
        out_shape=jax.ShapeDtypeStruct((8, 32, depth), BF),
        cost_estimate=LIGHT,
        name="cut_features",
    )(place, feats)


def partial_kernel(place, got_ref, swapped_ref, weight_ref, out_ref, rows):
    @pl.when(pl.program_id(0) == 0)
    def _():
        first = place[1] == 0
        got, swapped = got_ref[...], swapped_ref[...]
        rows[:, 0:32, :] = jnp.where(first, got, swapped)
        rows[:, 32:64, :] = jnp.where(first, swapped, got)

    lhs = rows[...].reshape(8 * IMG, rows.shape[2])
    value = jnp.dot(lhs, weight_ref[...], preferred_element_type=F32).astype(BF)
    out_ref[...] = value.reshape(8, IMG, value.shape[1])


def partial_images(place, got, swapped, weight):
    depth, width = weight.shape
    cut = width // 4
    rows = pl.BlockSpec((8, 32, depth), lambda i, place: (0, 0, 0))
    return pl.pallas_call(
        partial_kernel,
        grid_spec=pltpu.PrefetchScalarGridSpec(
            num_scalar_prefetch=1,
            grid=(4,),
            in_specs=[rows, rows, pl.BlockSpec((depth, cut), lambda i, place: (0, i))],
            out_specs=pl.BlockSpec((8, IMG, cut), lambda i, place: (0, 0, i)),
            scratch_shapes=[pltpu.VMEM((8, IMG, depth), BF)],
        ),
        out_shape=jax.ShapeDtypeStruct((8, IMG, width), BF),
        compiler_params=pltpu.CompilerParams(vmem_limit_bytes=VMEM_LIMIT),
        cost_estimate=LIGHT,
        name="partial_images",
    )(place, got, swapped, weight)


def image_kernel(
    place, pieces_ref, bias_ref, gain_ref, weight_ref, hidden_ref, swap_ref, same_ref, scaled, pair
):
    step = pl.program_id(0)

    @pl.when(step == 0)
    def _():
        total = pieces_ref[0].astype(F32)
        for k in range(1, 8):
            total = total + pieces_ref[k].astype(F32)
        total = total + bias_ref[...].astype(F32)
        image_hidden = (0.5 * total * (1.0 + lax.erf(total * (0.5**0.5)))).astype(BF)
        hidden_ref[...] = image_hidden
        hidden = image_hidden.astype(F32)
        scaled[...] = (hidden * gain_ref[...].astype(F32)).astype(BF)
        squared = hidden * hidden
        lanes = squared[:, 0:128]
        for k in range(1, 8):
            lanes = lanes + squared[:, k * 128 : (k + 1) * 128]
        lanes = jnp.concatenate([lanes, jnp.zeros_like(lanes)], axis=0)
        summed = jnp.sum(lanes.T, axis=0, keepdims=True)
        high, low = split_pair(summed)
        picked = lax.broadcasted_iota(jnp.int32, (16, 128), 0)
        rows = jnp.where(picked == 0, high.astype(F32), jnp.where(picked == 1, low.astype(F32), 0.0))
        pair[...] = jnp.concatenate([rows, jnp.zeros_like(rows)], axis=1).astype(BF)

    product = jnp.dot(scaled[...], weight_ref[...], preferred_element_type=F32)
    left, right = product[:, :256], product[:, 256:]
    first = place[1] == 0
    same_ref[0, 0:IMG, :] = jnp.where(first, left, right).astype(BF)
    swap_ref[0, 0:IMG, :] = jnp.where(first, right, left).astype(BF)
    same_ref[0, IMG:, :] = pair[...]
    swap_ref[0, IMG:, :] = pair[...]


def image_rows_kv(place, pieces, bias, gain, kv_w):
    def column(i, place):
        return (0, lax.rem(place[2] + i, 4))

    width = pieces.shape[2]
    row = pl.BlockSpec((1, width), lambda i, place: (0, 0))
    out = jax.ShapeDtypeStruct((4, IMG_TALL, 256), BF)
    return pl.pallas_call(
        image_kernel,
        grid_spec=pltpu.PrefetchScalarGridSpec(
            num_scalar_prefetch=1,
            grid=(4,),
            in_specs=[
                pl.BlockSpec((8, IMG, width), lambda i, place: (0, 0, 0)),
                row,
                row,
                pl.BlockSpec((width, 512), column),
            ],
            out_specs=[
                pl.BlockSpec((IMG, width), lambda i, place: (0, 0)),
                pl.BlockSpec((1, IMG_TALL, 256), lambda i, place: (i, 0, 0)),
                pl.BlockSpec((1, IMG_TALL, 256), lambda i, place: (i, 0, 0)),
            ],
            scratch_shapes=[pltpu.VMEM((IMG, width), BF), pltpu.VMEM((16, 256), BF)],
        ),
        out_shape=[jax.ShapeDtypeStruct((IMG, width), BF), out, out],
        compiler_params=pltpu.CompilerParams(vmem_limit_bytes=VMEM_LIMIT),
        cost_estimate=LIGHT,
        name="image_rows_kv",
    )(place, pieces, bias, gain, kv_w)


def pair_kernel(same_ref, received_ref, *out_refs):
    for j, out_ref in enumerate(out_refs):
        total = same_ref[j].astype(F32) + received_ref[j].astype(F32)
        out_ref[0:IMG, :] = total[0:IMG].astype(BF)
        high, low = split_pair(total[IMG : IMG + 1] + total[IMG + 1 : IMG + 2])
        picked = lax.broadcasted_iota(jnp.int32, (16, 256), 0)
        rows = jnp.where(picked == 0, high.astype(F32), jnp.where(picked == 1, low.astype(F32), 0.0))
        out_ref[IMG:, :] = rows.astype(BF)


def pair_images(same, received):
    return pl.pallas_call(
        pair_kernel,
        out_shape=[jax.ShapeDtypeStruct((IMG_TALL, 256), BF)] * 4,
        cost_estimate=LIGHT,
        name="pair_images",
    )(same, received)


def close_kernel(a_ref, b_ref, c_ref, d_ref, labels_ref, out_ref):
    total = a_ref[...].astype(F32) + b_ref[...].astype(F32)
    total = total + c_ref[...].astype(F32) + d_ref[...].astype(F32)
    squares = total[IMG : IMG + 1, 0:128] + total[IMG + 1 : IMG + 2, 0:128]
    scale = lax.rsqrt(squares / D + 1e-05)
    scale = jnp.where(labels_ref[3:4, 0:128].astype(F32) > 0.5, scale, 0.0)
    tile = jnp.broadcast_to(scale, (128, 128)).T[0:IMG]
    tile = jnp.concatenate([tile, tile], axis=1)
    out_ref[0:IMG, :] = jnp.where(tile > 0.0, total[0:IMG] * tile, 0.0).astype(BF)
    out_ref[IMG:, :] = labels_ref[...]


def close_images(parts, labels):
    return pl.pallas_call(
        close_kernel,
        out_shape=jax.ShapeDtypeStruct((IMG_TALL, 256), BF),
        cost_estimate=LIGHT,
        name="close_images",
    )(*parts, labels)


def merge_kernel(
    place, own_ref, other_ref, first_ref, second_ref, near_ref, yonder_ref, side_ref, far_ref, out_ref
):
    def one(k):
        step = 2 * pl.program_id(0) + k
        match = jnp.where(place[0] == 0, step, place[3]).astype(F32)
        shard = jnp.where(place[0] == 0, place[3], step)
        level = lax.rem(place[3] - shard + 8, 4)
        close = (shard >= 4) == (place[3] >= 4)
        images = []
        for near, away in ((near_ref, yonder_ref), (side_ref, far_ref)):
            images.append(jnp.where(close, near[level].astype(F32), away[level].astype(F32)))
        targets = []
        for image in images:
            owner = image[IMG : IMG + 1, 0:IMG]
            spot = image[IMG + 1 : IMG + 2, 0:IMG] * PAGE + image[IMG + 2 : IMG + 3, 0:IMG]
            targets.append(jnp.where(owner == match, spot, -1.0))
        target = jnp.concatenate(targets, axis=1)
        data = jnp.concatenate([images[0][0:IMG], images[1][0:IMG]], axis=0).astype(BF)
        spots = lax.broadcasted_iota(jnp.int32, (CAP * PAGE, 2 * IMG), 0).astype(F32)
        chosen = (spots == target).astype(F32).astype(BF)
        image = jnp.dot(chosen, data, preferred_element_type=F32)
        taken = jnp.dot(chosen, jnp.ones((2 * IMG, 128), BF), preferred_element_type=F32) > 0.5

        def write(left, right):
            for half, text in enumerate((left, right)):
                lanes = slice(half * 128, half * 128 + 128)
                text = text.reshape(CAP * PAGE, 128).astype(F32)
                merged = jnp.where(taken, image[:, lanes], text).astype(BF)
                out_ref[k * CAP : (k + 1) * CAP, :, lanes] = merged.reshape(CAP, PAGE, 128)

        @pl.when(place[0] == 0)
        def _():
            write(own_ref[0, k * CAP : (k + 1) * CAP], other_ref[k * CAP : (k + 1) * CAP])

        @pl.when(place[0] != 0)
        def _():
            write(first_ref[0, k * CAP : (k + 1) * CAP], second_ref[0, k * CAP : (k + 1) * CAP])

    one(0)
    one(1)


def merge_slots(place, own, other, arrived, images):
    def local(i, place):
        return jnp.where(place[0] == 0, i, 3)

    def remote(i, place):
        return jnp.where(place[0] == 0, 0, i)

    image_spec = pl.BlockSpec((4, IMG_TALL, 256), lambda i, place: (0, 0, 0))
    return pl.pallas_call(
        merge_kernel,
        grid_spec=pltpu.PrefetchScalarGridSpec(
            num_scalar_prefetch=1,
            grid=(4,),
            in_specs=[
                pl.BlockSpec((1, 2 * CAP, PAGE, 128), lambda i, place: (1, local(i, place), 0, 0)),
                pl.BlockSpec((2 * CAP, PAGE, 128), lambda i, place: (local(i, place), 0, 0)),
                pl.BlockSpec((1, 2 * CAP, PAGE, 128), lambda i, place: (0, remote(i, place), 0, 0)),
                pl.BlockSpec((1, 2 * CAP, PAGE, 128), lambda i, place: (1, remote(i, place), 0, 0)),
            ]
            + [image_spec] * 4,
            out_specs=pl.BlockSpec((2 * CAP, PAGE, 256), lambda i, place: (i, 0, 0)),
        ),
        out_shape=jax.ShapeDtypeStruct((256, PAGE, 256), BF),
        compiler_params=pltpu.CompilerParams(vmem_limit_bytes=VMEM_LIMIT),
        cost_estimate=LIGHT,
        name="merge_slots",
    )(place, own, other, arrived, arrived, *images)


def attend(queries, kv_cache, new_kv, cache_lengths):
    row_count = queries.shape[0]
    heads_kv = kv_cache.shape[2] // (2 * HEAD)
    grouped = queries.reshape(row_count, heads_kv, queries.shape[1] // (HEAD * heads_kv), HEAD)
    stored = kv_cache.reshape(row_count, kv_cache.shape[1], heads_kv, 2 * HEAD)
    fresh_kv = new_kv.reshape(row_count, heads_kv, 2 * HEAD)
    scores = jnp.einsum(
        "rgqh,rjgh->rgqj", grouped, stored[..., :HEAD], preferred_element_type=jnp.float32
    ) * HEAD ** (-0.5)
    in_cache = jnp.arange(stored.shape[1], dtype=jnp.int32)[None, :] < cache_lengths[:, None]
    scores = jnp.where(in_cache[:, None, None, :], scores, -1e30)
    own_score = jnp.einsum(
        "rgqh,rgh->rgq", grouped, fresh_kv[..., :HEAD], preferred_element_type=jnp.float32
    ) * HEAD ** (-0.5)
    row_max = jnp.maximum(jnp.max(scores, axis=3), own_score)
    weights = jnp.exp(scores - row_max[..., None])
    own_weight = jnp.exp(own_score - row_max)
    denominator = jnp.sum(weights, axis=3) + own_weight
    probability = (weights / denominator[..., None]).astype(jnp.bfloat16)
    own_prob = lax.optimization_barrier((own_weight / denominator).astype(jnp.bfloat16)).astype(
        jnp.float32
    )
    attended = jnp.einsum(
        "rgqj,rjgh->rgqh", probability, stored[..., HEAD:], preferred_element_type=jnp.float32
    )
    attended = attended + own_prob[..., None] * fresh_kv[:, :, None, HEAD:].astype(jnp.float32)
    return attended.astype(jnp.bfloat16).reshape(row_count, queries.shape[1])


PARTNER = [(i, i ^ 1) for i in range(8)]


def shift(k):
    return [(i, (i + 2 * k) % 8) for i in range(8)]


def seq_shift(y, z):
    return [(i, (i // 4 + y) % 2 * 4 + (i + z) % 4) for i in range(8)]


FAR = [(g * 8 + i, (1 - g) * 8 + (i + 4) % 8) for g in range(2) for i in range(8)]


def after(value, other):
    return lax.optimization_barrier((value, other))[0]


def per_device(
    embeds,
    image_feats,
    image_pos,
    proj_w,
    proj_b,
    norm_gain,
    kv_w,
    prompt_lengths,
    page_owner,
    queries,
    kv_cache,
    new_kv,
    cache_lengths,
):
    group = lax.axis_index("group").astype(jnp.int32)
    seq = lax.axis_index("seq").astype(jnp.int32)
    mp = lax.axis_index("mp").astype(jnp.int32)
    core, x = mp % 2, mp // 2
    place = jnp.stack([group, core, x, seq])
    gain = norm_gain.reshape(1, -1)

    bias = proj_b.reshape(1, -1)

    owners = page_owner[:, 0]
    before = (
        jnp.arange(PAGES, dtype=jnp.int32)[None, :] < jnp.arange(PAGES, dtype=jnp.int32)[:, None]
    )
    page_rank = jnp.sum((before & (owners[:, None] == owners[None, :])).astype(jnp.int32), axis=1)
    slots = owners * CAP + page_rank
    live = jnp.sum(jnp.where(jnp.arange(4, dtype=jnp.int32) == seq // 2, prompt_lengths, 0))
    limit = live - (seq % 2) * ROWS
    local_pos = lax.dynamic_slice(image_pos, (group * IMG,), (IMG,)) - seq * ROWS
    at_page = (local_pos // PAGE)[:, None] == jnp.arange(PAGES, dtype=jnp.int32)[None, :]
    image_owner = jnp.sum(jnp.where(at_page, owners[None, :], 0), axis=1)
    image_rank = jnp.sum(jnp.where(at_page, page_rank[None, :], 0), axis=1)
    labels = jnp.stack(
        [image_owner, image_rank, local_pos % PAGE, (local_pos < limit).astype(jnp.int32)]
    ).astype(BF)
    labels = jnp.pad(labels, ((0, 12), (0, 256 - IMG)))

    got = lax.all_to_all(cut_features(place, image_feats), "seq", 0, 0, tiled=True)

    send, keep = project_text(place, embeds, gain, kv_w)
    got = after(got, keep[0])
    swapped = lax.ppermute(got, "mp", PARTNER)
    received = [lax.ppermute(piece, "mp", PARTNER) for piece in send]
    added = [None] + [add_pair(keep[j], received[j]) for j in (1, 2, 3)]
    parts = [keep[0], received[0]] + [lax.ppermute(added[j], "mp", shift(j)) for j in (1, 2, 3)]

    partial = partial_images(place, got, after(swapped, added[1:]), proj_w)
    attended = lax.cond(
        group != 0,
        attend,
        lambda *unused: jnp.zeros(queries.shape, BF),
        after(queries, partial),
        kv_cache,
        new_kv,
        cache_lengths,
    )
    pieces = lax.all_to_all(partial, "seq", 0, 0, tiled=True)
    image_hidden, swap, same = image_rows_kv(place, pieces, bias, gain, kv_w)
    image_pairs = pair_images(same, lax.ppermute(swap, "mp", PARTNER))
    image_parts = [image_pairs[0]]
    image_parts += [lax.ppermute(image_pairs[j], "mp", shift(j)) for j in (1, 2, 3)]

    rows, by_owner = finish_text(slots, after(limit.reshape(1), attended), parts)
    other_rows = lax.ppermute(rows, "group", [(1, 0)])
    arrived = lax.all_to_all(
        by_owner.reshape(512, PAGE, 128), ("group", "seq"), split_axis=0, concat_axis=0, tiled=True
    ).reshape(2, 256, PAGE, 128)

    image_parts = after(image_parts, by_owner)
    image_block = close_images(image_parts, labels)
    near = jnp.stack(
        [image_block] + [lax.ppermute(image_block, "seq", seq_shift(0, k)) for k in (1, 2, 3)]
    )
    images = [
        near,
        lax.ppermute(near, "seq", seq_shift(1, 0)),
        lax.ppermute(near, "group", [(0, 1), (1, 0)]),
        lax.ppermute(near, ("group", "seq"), FAR),
    ]
    other = place_pages(slots, other_rows)
    page_slots = merge_slots(place, by_owner, other, arrived, images)

    other_hidden = lax.ppermute(image_hidden, "group", [(1, 0)])
    row_states = jnp.where(
        group == 0, jnp.concatenate([image_hidden, other_hidden], axis=0), attended
    )
    return (page_slots, row_states)


def solution(mesh):
    in_specs = (
        P("seq", "mp"),
        P("seq", None),
        P("seq"),
        P("seq", "mp"),
        P("mp"),
        P("mp"),
        P("mp", None),
        P(),
        P("seq", None),
        P("seq", "mp"),
        P("seq", None, "mp"),
        P("seq", "mp"),
        P("seq"),
    )
    out_specs = (P(("group", "seq"), None, "mp"), P(("group", "seq"), "mp"))
    return jax.shard_map(
        per_device, mesh=mesh, in_specs=in_specs, out_specs=out_specs, check_vma=False
    )
```

```python
import functools

import jax
import jax.numpy as jnp
from jax import lax
from jax.experimental import pallas as pl
from jax.experimental.pallas import tpu as pltpu
from jax.sharding import PartitionSpec as P

D = 8192
HEAD = 128
PAGE = 16
PROMPT_LEN = 4096
CAP = 32
ROWS = 2048
EXT = 32
TALL = ROWS + EXT
PAGES = ROWS // PAGE
IMG = 64
IMG_TALL = IMG + 16
BF = jnp.bfloat16
F32 = jnp.float32
def work(micros):
    size = int(micros * 3700000)
    return pl.CostEstimate(flops=micros * 1000000, bytes_accessed=size, transcendentals=0)


LIGHT = pl.CostEstimate(flops=1, bytes_accessed=1, transcendentals=0)
VMEM_LIMIT = 56 * 1024 * 1024


def split_pair(value):
    high = value.astype(BF)
    low = (value - high.astype(F32)).astype(BF)
    return high, low


TILE = 512
STEPS = ROWS // TILE


def project_kernel(place, embeds_ref, gain_ref, *refs):
    weights, send, keep, squares_ref = refs[0:8], refs[8:12], refs[12:16], refs[16]
    step = pl.program_id(0)

    @pl.when(step < STEPS)
    def _():
        hidden = embeds_ref[...].astype(F32)
        scaled = (hidden * gain_ref[...].astype(F32).reshape(1, -1)).astype(BF)
        squared = hidden * hidden
        lanes = squared[:, 0:128]
        for k in range(1, 8):
            lanes = lanes + squared[:, k * 128 : (k + 1) * 128]
        summed = jnp.sum(lanes.T, axis=0, keepdims=True)
        for k in range(TILE // 128):
            squares_ref[pl.ds(TILE // 128 * step + k, 1), :] = summed[:, k * 128 : (k + 1) * 128]
        for k, target in enumerate((send[:2], send[2:], keep[:2], keep[2:])):
            weight = jnp.concatenate([weights[2 * k][...], weights[2 * k + 1][...]], axis=1)
            product = jnp.dot(scaled, weight, preferred_element_type=F32).astype(BF)
            target[0][...] = product[:, :128]
            target[1][...] = product[:, 128:]

    @pl.when(step == STEPS)
    def _():
        high, low = split_pair(squares_ref[...])
        both = jnp.concatenate([high, low], axis=0)
        for ref in (*send, *keep):
            ref[0:EXT, :] = both


def project_text(place, embeds, gain, kv_w):
    def column(r, j):
        def index(i, place):
            core = place[1] if r else 1 - place[1]
            head = 2 * lax.rem(place[2] + j, 4) + core
            return (0, 2 * head + place[0])

        return index

    specs = [
        pl.BlockSpec((TILE, 1024), lambda i, place: (jnp.minimum(i, STEPS - 1), 0)),
        pl.BlockSpec((1024,), lambda i, place: (0,)),
    ] + [pl.BlockSpec((1024, 128), column(r, j)) for r in range(2) for j in range(4)]
    outs = pl.pallas_call(
        project_kernel,
        grid_spec=pltpu.PrefetchScalarGridSpec(
            num_scalar_prefetch=1,
            grid=(STEPS + 1,),
            in_specs=specs,
            out_specs=[pl.BlockSpec((TILE, 128), lambda i, place: (i, 0))] * 8,
            scratch_shapes=[pltpu.VMEM((16, 128), F32)],
        ),
        out_shape=[jax.ShapeDtypeStruct((TALL, 128), BF)] * 8,
        compiler_params=pltpu.CompilerParams(vmem_limit_bytes=VMEM_LIMIT),
        cost_estimate=LIGHT,
        name="project_text",
    )(place, embeds, gain, *([kv_w] * 8))
    return outs[:4], outs[4:]


def square_rows(refs):
    total = jnp.zeros((16, 128), F32)
    for ref in refs:
        total = total + ref[ROWS : ROWS + 16, :].astype(F32) + ref[ROWS + 16 : TALL, :].astype(F32)
    return total


def add_pair(keep, received):
    return (keep.astype(F32) + received.astype(F32)).astype(BF)


def finish_kernel(slots, mask_ref, *refs):
    parts, (rows_ref, slot_ref) = refs[:5], refs[5:]
    slot_ref[...] = jnp.zeros_like(slot_ref)
    squares = square_rows(parts)
    scale = jnp.where(mask_ref[...] > 0.0, lax.rsqrt(squares / D + 1e-05), 0.0)
    for part in range(16):
        tile = jnp.broadcast_to(scale[part : part + 1, :], (128, 128)).T
        here = slice(part * 128, part * 128 + 128)
        total = parts[0][here, :].astype(F32)
        for ref in parts[1:]:
            total = total + ref[here, :].astype(F32)
        rows = jnp.where(tile > 0.0, total * tile, 0.0).astype(BF)
        for p in range(8):
            page = rows[p * PAGE : (p + 1) * PAGE, :]
            rows_ref[part * 8 + p] = page
            slot_ref[0, slots[part * 8 + p]] = page


def finish_text(slots, mask, parts):
    whole = lambda i, slots: (0, 0)
    return pl.pallas_call(
        finish_kernel,
        grid_spec=pltpu.PrefetchScalarGridSpec(
            num_scalar_prefetch=1,
            grid=(1,),
            in_specs=[pl.BlockSpec((16, 128), whole)] + [pl.BlockSpec((TALL, 128), whole)] * 5,
            out_specs=[
                pl.BlockSpec((PAGES, PAGE, 128), lambda i, slots: (0, 0, 0)),
                pl.BlockSpec((1, 256, PAGE, 128), lambda i, slots: (1, 0, 0, 0)),
            ],
        ),
        out_shape=[
            jax.ShapeDtypeStruct((PAGES, PAGE, 128), BF),
            jax.ShapeDtypeStruct((2, 256, PAGE, 128), BF),
        ],
        compiler_params=pltpu.CompilerParams(vmem_limit_bytes=VMEM_LIMIT),
        cost_estimate=work(20000),
        name="finish_text",
    )(slots, mask, *parts)


def cut_kernel(place, feats_ref, out_ref):
    depth = out_ref.shape[2]
    for k in range(8):
        out_ref[k] = feats_ref[:, k * depth : (k + 1) * depth]


def cut_features(place, feats):
    depth = feats.shape[1] // 8
    return pl.pallas_call(
        cut_kernel,
        grid_spec=pltpu.PrefetchScalarGridSpec(
            num_scalar_prefetch=1,
            grid=(1,),
            in_specs=[
                pl.BlockSpec((32, feats.shape[1]), lambda i, place: (2 * place[0] + place[1], 0))
            ],
            out_specs=pl.BlockSpec((8, 32, depth), lambda i, place: (0, 0, 0)),
        ),
        out_shape=jax.ShapeDtypeStruct((8, 32, depth), BF),
        cost_estimate=LIGHT,
        name="cut_features",
    )(place, feats)


def image_kernel(
    place, pieces_ref, bias_ref, gain_ref, weight_ref, hidden_ref, swap_ref, same_ref, scaled, pair
):
    step = pl.program_id(0)

    @pl.when(step == 0)
    def _():
        total = pieces_ref[0].astype(F32)
        for k in range(1, 8):
            total = total + pieces_ref[k].astype(F32)
        flipped = jnp.concatenate([total[32:64], total[0:32]], axis=0)
        total = jnp.where(place[1] == 0, total, flipped)
        total = total + bias_ref[...].astype(F32).reshape(1, -1)
        image_hidden = (0.5 * total * (1.0 + lax.erf(total * (0.5**0.5)))).astype(BF)
        hidden_ref[...] = image_hidden
        hidden = image_hidden.astype(F32)
        scaled[...] = (hidden * gain_ref[...].astype(F32).reshape(1, -1)).astype(BF)
        squared = hidden * hidden
        lanes = squared[:, 0:128]
        for k in range(1, 8):
            lanes = lanes + squared[:, k * 128 : (k + 1) * 128]
        lanes = jnp.concatenate([lanes, jnp.zeros_like(lanes)], axis=0)
        summed = jnp.sum(lanes.T, axis=0, keepdims=True)
        high, low = split_pair(summed)
        picked = lax.broadcasted_iota(jnp.int32, (16, 128), 0)
        rows = jnp.where(picked == 0, high.astype(F32), jnp.where(picked == 1, low.astype(F32), 0.0))
        pair[...] = jnp.concatenate([rows, jnp.zeros_like(rows)], axis=1).astype(BF)

    product = jnp.dot(scaled[...], weight_ref[...], preferred_element_type=F32)
    left, right = product[:, :256], product[:, 256:]
    first = place[1] == 0
    same_ref[0, 0:IMG, :] = jnp.where(first, left, right).astype(BF)
    swap_ref[0, 0:IMG, :] = jnp.where(first, right, left).astype(BF)
    same_ref[0, IMG:, :] = pair[...]
    swap_ref[0, IMG:, :] = pair[...]


def image_rows_kv(place, pieces, bias, gain, kv_w):
    def column(i, place):
        return (0, lax.rem(place[2] + i, 4))

    width = pieces.shape[2]
    row = pl.BlockSpec((width,), lambda i, place: (0,))
    out = jax.ShapeDtypeStruct((4, IMG_TALL, 256), BF)
    return pl.pallas_call(
        image_kernel,
        grid_spec=pltpu.PrefetchScalarGridSpec(
            num_scalar_prefetch=1,
            grid=(4,),
            in_specs=[
                pl.BlockSpec((8, IMG, width), lambda i, place: (0, 0, 0)),
                row,
                row,
                pl.BlockSpec((width, 512), column),
            ],
            out_specs=[
                pl.BlockSpec((IMG, width), lambda i, place: (0, 0)),
                pl.BlockSpec((1, IMG_TALL, 256), lambda i, place: (i, 0, 0)),
                pl.BlockSpec((1, IMG_TALL, 256), lambda i, place: (i, 0, 0)),
            ],
            scratch_shapes=[pltpu.VMEM((IMG, width), BF), pltpu.VMEM((16, 256), BF)],
        ),
        out_shape=[jax.ShapeDtypeStruct((IMG, width), BF), out, out],
        compiler_params=pltpu.CompilerParams(vmem_limit_bytes=VMEM_LIMIT),
        cost_estimate=LIGHT,
        name="image_rows_kv",
    )(place, pieces, bias, gain, kv_w)


def close_kernel(a_ref, b_ref, c_ref, d_ref, labels_ref, out_ref):
    total = a_ref[...].astype(F32) + b_ref[...].astype(F32)
    total = total + c_ref[...].astype(F32) + d_ref[...].astype(F32)
    squares = total[IMG : IMG + 1, 0:128] + total[IMG + 1 : IMG + 2, 0:128]
    scale = lax.rsqrt(squares / D + 1e-05)
    scale = jnp.where(labels_ref[3:4, 0:128].astype(F32) > 0.5, scale, 0.0)
    tile = jnp.broadcast_to(scale, (128, 128)).T[0:IMG]
    tile = jnp.concatenate([tile, tile], axis=1)
    out_ref[0:IMG, :] = jnp.where(tile > 0.0, total[0:IMG] * tile, 0.0).astype(BF)
    out_ref[IMG:, :] = labels_ref[...]


def close_images(parts, labels):
    return pl.pallas_call(
        close_kernel,
        out_shape=jax.ShapeDtypeStruct((IMG_TALL, 256), BF),
        cost_estimate=LIGHT,
        name="close_images",
    )(*parts, labels)


def merge_kernel(
    place, slots, own_ref, rows_ref, first_ref, second_ref, near_ref, yonder_ref, side_ref, far_ref, out_ref, other
):
    prefill = place[0] == 0

    @pl.when(jnp.logical_and(prefill, pl.program_id(0) == 0))
    def _():
        other[...] = jnp.zeros_like(other)
        for p in range(PAGES):
            other[slots[p]] = rows_ref[p]

    def one(k):
        step = 2 * pl.program_id(0) + k
        match = jnp.where(prefill, step, place[3]).astype(F32)
        shard = jnp.where(prefill, place[3], step)
        level = lax.rem(place[3] - shard + 8, 4)
        close = (shard >= 4) == (place[3] >= 4)
        images = []
        for near, away in ((near_ref, yonder_ref), (side_ref, far_ref)):
            images.append(jnp.where(close, near[level], away[level]))
        targets = []
        for image in images:
            labels = image[IMG:IMG_TALL, 0:IMG].astype(F32)
            spot = labels[1:2] * PAGE + labels[2:3]
            targets.append(jnp.where(labels[0:1] == match, spot, -1.0))
        target = jnp.concatenate(targets, axis=1)
        data = jnp.concatenate([images[0][0:IMG], images[1][0:IMG]], axis=0)
        spots = lax.broadcasted_iota(jnp.int32, (CAP * PAGE, 2 * IMG), 0).astype(F32)
        chosen = (spots == target).astype(F32).astype(BF)
        image = jnp.dot(chosen, data, preferred_element_type=F32).astype(BF)

        def write(left, right):
            for half, text in enumerate((left, right)):
                lanes = slice(half * 128, half * 128 + 128)
                text = text.reshape(CAP * PAGE, 128)
                out_ref[k * CAP : (k + 1) * CAP, :, lanes] = (text + image[:, lanes]).reshape(CAP, PAGE, 128)

        @pl.when(prefill)
        def _():
            here = pl.ds(step * CAP, CAP)
            write(own_ref[0, k * CAP : (k + 1) * CAP], other[here])

        @pl.when(jnp.logical_not(prefill))
        def _():
            write(first_ref[0, k * CAP : (k + 1) * CAP], second_ref[0, k * CAP : (k + 1) * CAP])

    one(0)
    one(1)


def merge_slots(place, slots, own, rows, arrived, images):
    def local(i, place):
        return jnp.where(place[0] == 0, i, 3)

    def remote(i, place):
        return jnp.where(place[0] == 0, 0, i)

    image_spec = pl.BlockSpec((4, IMG_TALL, 256), lambda i, place, slots: (0, 0, 0))
    chunk = (1, 2 * CAP, PAGE, 128)
    return pl.pallas_call(
        merge_kernel,
        grid_spec=pltpu.PrefetchScalarGridSpec(
            num_scalar_prefetch=2,
            grid=(4,),
            in_specs=[
                pl.BlockSpec(chunk, lambda i, place, slots: (1, local(i, place), 0, 0)),
                pl.BlockSpec((PAGES, PAGE, 128), lambda i, place, slots: (0, 0, 0)),
                pl.BlockSpec(chunk, lambda i, place, slots: (0, remote(i, place), 0, 0)),
                pl.BlockSpec(chunk, lambda i, place, slots: (1, remote(i, place), 0, 0)),
            ]
            + [image_spec] * 4,
            out_specs=pl.BlockSpec((2 * CAP, PAGE, 256), lambda i, place, slots: (i, 0, 0)),
            scratch_shapes=[pltpu.VMEM((256, PAGE, 128), BF)],
        ),
        out_shape=jax.ShapeDtypeStruct((256, PAGE, 256), BF),
        compiler_params=pltpu.CompilerParams(vmem_limit_bytes=VMEM_LIMIT),
        cost_estimate=LIGHT,
        name="merge_slots",
    )(place, slots, own, rows, arrived, arrived, *images)


def attend(queries, kv_cache, new_kv, cache_lengths):
    row_count = queries.shape[0]
    heads_kv = kv_cache.shape[2] // (2 * HEAD)
    grouped = queries.reshape(row_count, heads_kv, queries.shape[1] // (HEAD * heads_kv), HEAD)
    stored = kv_cache.reshape(row_count, kv_cache.shape[1], heads_kv, 2 * HEAD)
    fresh_kv = new_kv.reshape(row_count, heads_kv, 2 * HEAD)
    scores = jnp.einsum(
        "rgqh,rjgh->rgqj", grouped, stored[..., :HEAD], preferred_element_type=jnp.float32
    ) * HEAD ** (-0.5)
    in_cache = jnp.arange(stored.shape[1], dtype=jnp.int32)[None, :] < cache_lengths[:, None]
    scores = jnp.where(in_cache[:, None, None, :], scores, -1e30)
    own_score = jnp.einsum(
        "rgqh,rgh->rgq", grouped, fresh_kv[..., :HEAD], preferred_element_type=jnp.float32
    ) * HEAD ** (-0.5)
    row_max = jnp.maximum(jnp.max(scores, axis=3), own_score)
    weights = jnp.exp(scores - row_max[..., None])
    own_weight = jnp.exp(own_score - row_max)
    denominator = jnp.sum(weights, axis=3) + own_weight
    probability = (weights / denominator[..., None]).astype(jnp.bfloat16)
    own_prob = lax.optimization_barrier((own_weight / denominator).astype(jnp.bfloat16)).astype(
        jnp.float32
    )
    attended = jnp.einsum(
        "rgqj,rjgh->rgqh", probability, stored[..., HEAD:], preferred_element_type=jnp.float32
    )
    attended = attended + own_prob[..., None] * fresh_kv[:, :, None, HEAD:].astype(jnp.float32)
    return attended.astype(jnp.bfloat16).reshape(row_count, queries.shape[1])


PARTNER = [(i, i ^ 1) for i in range(8)]


def shift(k):
    return [(i, (i + 2 * k) % 8) for i in range(8)]


def seq_shift(y, z):
    return [(i, (i // 4 + y) % 2 * 4 + (i + z) % 4) for i in range(8)]


FAR = [(g * 8 + i, (1 - g) * 8 + (i + 4) % 8) for g in range(2) for i in range(8)]


def after(value, other):
    return lax.optimization_barrier((value, other))[0]


def per_device(
    embeds,
    image_feats,
    image_pos,
    proj_w,
    proj_b,
    norm_gain,
    kv_w,
    prompt_lengths,
    page_owner,
    queries,
    kv_cache,
    new_kv,
    cache_lengths,
):
    group = lax.axis_index("group").astype(jnp.int32)
    seq = lax.axis_index("seq").astype(jnp.int32)
    mp = lax.axis_index("mp").astype(jnp.int32)
    core, x = mp % 2, mp // 2
    place = jnp.stack([group, core, x, seq])


    owners = page_owner[:, 0]
    before = (
        jnp.arange(PAGES, dtype=jnp.int32)[None, :] < jnp.arange(PAGES, dtype=jnp.int32)[:, None]
    )
    page_rank = jnp.sum((before & (owners[:, None] == owners[None, :])).astype(jnp.int32), axis=1)
    slots = owners * CAP + page_rank
    live = jnp.sum(jnp.where(jnp.arange(4, dtype=jnp.int32) == seq // 2, prompt_lengths, 0))
    limit = live - (seq % 2) * ROWS
    local_pos = lax.dynamic_slice(image_pos, (group * IMG,), (IMG,)) - seq * ROWS
    at_page = (local_pos // PAGE)[:, None] == jnp.arange(PAGES, dtype=jnp.int32)[None, :]
    image_owner = jnp.sum(jnp.where(at_page, owners[None, :], 0), axis=1)
    image_rank = jnp.sum(jnp.where(at_page, page_rank[None, :], 0), axis=1)
    labels = jnp.stack(
        [image_owner, image_rank, local_pos % PAGE, (local_pos < limit).astype(jnp.int32)]
    ).astype(BF)
    tokens = jnp.arange(ROWS, dtype=jnp.int32).reshape(16, 128)
    places = image_pos - seq * ROWS
    upper = (places // 128)[None, :] == jnp.arange(16, dtype=jnp.int32)[:, None]
    lower = (places % 128)[:, None] == jnp.arange(128, dtype=jnp.int32)[None, :]
    is_image = jnp.dot(upper.astype(BF), lower.astype(BF), preferred_element_type=F32)
    mask = jnp.where((tokens < limit) & (is_image < 0.5), 1.0, 0.0).astype(F32)
    labels = jnp.pad(labels, ((0, 12), (0, 256 - IMG)))

    got = lax.all_to_all(cut_features(place, image_feats), "seq", 0, 0, tiled=True)

    send, keep = project_text(place, embeds, norm_gain, kv_w)
    got = after(got, keep[0])
    swapped = lax.ppermute(got, "mp", PARTNER)
    received = [lax.ppermute(piece, "mp", PARTNER) for piece in send]
    added = [None] + [add_pair(keep[j], received[j]) for j in (1, 2, 3)]
    parts = [keep[0], received[0]] + [lax.ppermute(added[j], "mp", shift(j)) for j in (1, 2, 3)]

    feats = jnp.concatenate([got, after(swapped, added[1:])], axis=1).reshape(8 * IMG, -1)
    partial = jnp.dot(feats, proj_w, preferred_element_type=F32).astype(BF).reshape(8, IMG, -1)
    attended = lax.cond(
        group != 0,
        attend,
        lambda *unused: jnp.zeros(queries.shape, BF),
        after(queries, partial),
        kv_cache,
        new_kv,
        cache_lengths,
    )
    pieces = lax.all_to_all(partial, "seq", 0, 0, tiled=True)
    image_hidden, swap, same = image_rows_kv(place, pieces, proj_b, norm_gain, kv_w)
    image_pairs = add_pair(same, lax.ppermute(swap, "mp", PARTNER))
    image_parts = [image_pairs[0]]
    image_parts += [lax.ppermute(image_pairs[j], "mp", shift(j)) for j in (1, 2, 3)]

    rows, by_owner = finish_text(slots, after(mask, attended), parts)
    other_rows = lax.ppermute(rows, "group", [(1, 0)])
    arrived = lax.all_to_all(
        by_owner.reshape(512, PAGE, 128), ("group", "seq"), split_axis=0, concat_axis=0, tiled=True
    ).reshape(2, 256, PAGE, 128)

    image_parts = after(image_parts, by_owner)
    image_block = close_images(image_parts, labels)
    near = jnp.stack(
        [image_block] + [lax.ppermute(image_block, "seq", seq_shift(0, k)) for k in (1, 2, 3)]
    )
    images = [
        near,
        lax.ppermute(near, "seq", seq_shift(1, 0)),
        lax.ppermute(near, "group", [(0, 1), (1, 0)]),
        lax.ppermute(near, ("group", "seq"), FAR),
    ]
    page_slots = merge_slots(place, slots, by_owner, other_rows, arrived, images)

    other_hidden = lax.ppermute(image_hidden, "group", [(1, 0)])
    row_states = jnp.where(
        group == 0, jnp.concatenate([image_hidden, other_hidden], axis=0), attended
    )
    return (page_slots, row_states)


def solution(mesh):
    in_specs = (
        P("seq", "mp"),
        P("seq", None),
        P("seq"),
        P("seq", "mp"),
        P("mp"),
        P("mp"),
        P("mp", None),
        P(),
        P("seq", None),
        P("seq", "mp"),
        P("seq", None, "mp"),
        P("seq", "mp"),
        P("seq"),
    )
    out_specs = (P(("group", "seq"), None, "mp"), P(("group", "seq"), "mp"))
    return jax.shard_map(
        per_device, mesh=mesh, in_specs=in_specs, out_specs=out_specs, check_vma=False
    )
```

```python
import functools

import jax
import jax.numpy as jnp
from jax import lax
from jax.experimental import pallas as pl
from jax.experimental.pallas import tpu as pltpu
from jax.sharding import PartitionSpec as P

D = 8192
HEAD = 128
PAGE = 16
PROMPT_LEN = 4096
CAP = 32
ROWS = 2048
EXT = 32
TALL = ROWS + EXT
PAGES = ROWS // PAGE
IMG = 64
IMG_TALL = IMG + 16
BF = jnp.bfloat16
F32 = jnp.float32
def work(micros):
    size = int(micros * 3700000)
    return pl.CostEstimate(flops=micros * 1000000, bytes_accessed=size, transcendentals=0)


LIGHT = pl.CostEstimate(flops=1, bytes_accessed=1, transcendentals=0)
VMEM_LIMIT = 56 * 1024 * 1024


def split_pair(value):
    high = value.astype(BF)
    low = (value - high.astype(F32)).astype(BF)
    return high, low


TILE = 512
STEPS = ROWS // TILE


def project_kernel(place, embeds_ref, gain_ref, *refs):
    weights, send, keep, squares_ref = refs[0:8], refs[8:12], refs[12:16], refs[16]
    step = pl.program_id(0)

    @pl.when(step < STEPS)
    def _():
        hidden = embeds_ref[...].astype(F32)
        scaled = (hidden * gain_ref[...].astype(F32).reshape(1, -1)).astype(BF)
        squared = hidden * hidden
        lanes = squared[:, 0:128]
        for k in range(1, 8):
            lanes = lanes + squared[:, k * 128 : (k + 1) * 128]
        summed = jnp.sum(lanes.T, axis=0, keepdims=True)
        for k in range(TILE // 128):
            squares_ref[pl.ds(TILE // 128 * step + k, 1), :] = summed[:, k * 128 : (k + 1) * 128]
        for k, target in enumerate((send[:2], send[2:], keep[:2], keep[2:])):
            weight = jnp.concatenate([weights[2 * k][...], weights[2 * k + 1][...]], axis=1)
            product = jnp.dot(scaled, weight, preferred_element_type=F32).astype(BF)
            target[0][...] = product[:, :128]
            target[1][...] = product[:, 128:]

    @pl.when(step == STEPS)
    def _():
        high, low = split_pair(squares_ref[...])
        both = jnp.concatenate([high, low], axis=0)
        for ref in (*send, *keep):
            ref[0:EXT, :] = both


def project_text(place, embeds, gain, kv_w):
    def column(r, j):
        def index(i, place):
            core = place[1] if r else 1 - place[1]
            head = 2 * lax.rem(place[2] + j, 4) + core
            return (0, 2 * head + place[0])

        return index

    specs = [
        pl.BlockSpec((TILE, 1024), lambda i, place: (jnp.minimum(i, STEPS - 1), 0)),
        pl.BlockSpec((1024,), lambda i, place: (0,)),
    ] + [pl.BlockSpec((1024, 128), column(r, j)) for r in range(2) for j in range(4)]
    outs = pl.pallas_call(
        project_kernel,
        grid_spec=pltpu.PrefetchScalarGridSpec(
            num_scalar_prefetch=1,
            grid=(STEPS + 1,),
            in_specs=specs,
            out_specs=[pl.BlockSpec((TILE, 128), lambda i, place: (i, 0))] * 8,
            scratch_shapes=[pltpu.VMEM((16, 128), F32)],
        ),
        out_shape=[jax.ShapeDtypeStruct((TALL, 128), BF)] * 8,
        compiler_params=pltpu.CompilerParams(vmem_limit_bytes=VMEM_LIMIT),
        cost_estimate=LIGHT,
        name="project_text",
    )(place, embeds, gain, *([kv_w] * 8))
    return outs[:4], outs[4:]


def square_rows(refs):
    total = jnp.zeros((16, 128), F32)
    for ref in refs:
        total = total + ref[ROWS : ROWS + 16, :].astype(F32) + ref[ROWS + 16 : TALL, :].astype(F32)
    return total


def add_pair(keep, received):
    return (keep.astype(F32) + received.astype(F32)).astype(BF)


def finish_kernel(slots, mask_ref, *refs):
    parts, (rows_ref, slot_ref) = refs[:4], refs[4:]
    slot_ref[...] = jnp.zeros_like(slot_ref)
    squares = square_rows(parts)
    scale = jnp.where(mask_ref[...] > 0.0, lax.rsqrt(squares / D + 1e-05), 0.0)
    for part in range(16):
        tile = jnp.broadcast_to(scale[part : part + 1, :], (128, 128)).T
        here = slice(part * 128, part * 128 + 128)
        total = parts[0][here, :].astype(F32)
        for ref in parts[1:]:
            total = total + ref[here, :].astype(F32)
        rows = jnp.where(tile > 0.0, total * tile, 0.0).astype(BF)
        for p in range(8):
            page = rows[p * PAGE : (p + 1) * PAGE, :]
            rows_ref[part * 8 + p] = page
            slot_ref[0, slots[part * 8 + p]] = page


def finish_text(slots, mask, parts):
    whole = lambda i, slots: (0, 0)
    return pl.pallas_call(
        finish_kernel,
        grid_spec=pltpu.PrefetchScalarGridSpec(
            num_scalar_prefetch=1,
            grid=(1,),
            in_specs=[pl.BlockSpec((16, 128), whole)] + [pl.BlockSpec((TALL, 128), whole)] * 4,
            out_specs=[
                pl.BlockSpec((PAGES, PAGE, 128), lambda i, slots: (0, 0, 0)),
                pl.BlockSpec((1, 256, PAGE, 128), lambda i, slots: (1, 0, 0, 0)),
            ],
        ),
        out_shape=[
            jax.ShapeDtypeStruct((PAGES, PAGE, 128), BF),
            jax.ShapeDtypeStruct((2, 256, PAGE, 128), BF),
        ],
        compiler_params=pltpu.CompilerParams(vmem_limit_bytes=VMEM_LIMIT),
        cost_estimate=work(20000),
        name="finish_text",
    )(slots, mask, *parts)


def cut_kernel(place, feats_ref, out_ref):
    depth = out_ref.shape[2]
    for k in range(8):
        out_ref[k] = feats_ref[:, k * depth : (k + 1) * depth]


def cut_features(place, feats):
    depth = feats.shape[1] // 8
    return pl.pallas_call(
        cut_kernel,
        grid_spec=pltpu.PrefetchScalarGridSpec(
            num_scalar_prefetch=1,
            grid=(1,),
            in_specs=[
                pl.BlockSpec((32, feats.shape[1]), lambda i, place: (2 * place[0] + place[1], 0))
            ],
            out_specs=pl.BlockSpec((8, 32, depth), lambda i, place: (0, 0, 0)),
        ),
        out_shape=jax.ShapeDtypeStruct((8, 32, depth), BF),
        cost_estimate=LIGHT,
        name="cut_features",
    )(place, feats)


def image_kernel(
    place, pieces_ref, bias_ref, gain_ref, weight_ref, hidden_ref, heads_ref, scaled, pair
):
    step = pl.program_id(0)

    @pl.when(step == 0)
    def _():
        total = pieces_ref[0].astype(F32)
        for k in range(1, 8):
            total = total + pieces_ref[k].astype(F32)
        flipped = jnp.concatenate([total[32:64], total[0:32]], axis=0)
        total = jnp.where(place[1] == 0, total, flipped)
        total = total + bias_ref[...].astype(F32).reshape(1, -1)
        image_hidden = (0.5 * total * (1.0 + lax.erf(total * (0.5**0.5)))).astype(BF)
        hidden_ref[...] = image_hidden
        hidden = image_hidden.astype(F32)
        scaled[...] = (hidden * gain_ref[...].astype(F32).reshape(1, -1)).astype(BF)
        squared = hidden * hidden
        lanes = squared[:, 0:128]
        for k in range(1, 8):
            lanes = lanes + squared[:, k * 128 : (k + 1) * 128]
        lanes = jnp.concatenate([lanes, jnp.zeros_like(lanes)], axis=0)
        summed = jnp.sum(lanes.T, axis=0, keepdims=True)
        high, low = split_pair(summed)
        picked = lax.broadcasted_iota(jnp.int32, (16, 128), 0)
        rows = jnp.where(picked == 0, high.astype(F32), jnp.where(picked == 1, low.astype(F32), 0.0))
        pair[...] = jnp.concatenate([rows, jnp.zeros_like(rows)], axis=1).astype(BF)

    product = jnp.dot(scaled[...], weight_ref[...], preferred_element_type=F32)
    for k in range(2):
        heads_ref[k, 0:IMG, :] = product[:, 256 * k : 256 * (k + 1)].astype(BF)
        heads_ref[k, IMG:, :] = pair[...]


def image_rows_kv(place, pieces, bias, gain, kv_w):
    width = pieces.shape[2]
    row = pl.BlockSpec((width,), lambda i, place: (0,))
    return pl.pallas_call(
        image_kernel,
        grid_spec=pltpu.PrefetchScalarGridSpec(
            num_scalar_prefetch=1,
            grid=(4,),
            in_specs=[
                pl.BlockSpec((8, IMG, width), lambda i, place: (0, 0, 0)),
                row,
                row,
                pl.BlockSpec((width, 512), lambda i, place: (0, i)),
            ],
            out_specs=[
                pl.BlockSpec((IMG, width), lambda i, place: (0, 0)),
                pl.BlockSpec((2, IMG_TALL, 256), lambda i, place: (i, 0, 0)),
            ],
            scratch_shapes=[pltpu.VMEM((IMG, width), BF), pltpu.VMEM((16, 256), BF)],
        ),
        out_shape=[
            jax.ShapeDtypeStruct((IMG, width), BF),
            jax.ShapeDtypeStruct((8, IMG_TALL, 256), BF),
        ],
        compiler_params=pltpu.CompilerParams(vmem_limit_bytes=VMEM_LIMIT),
        cost_estimate=LIGHT,
        name="image_rows_kv",
    )(place, pieces, bias, gain, kv_w)


def close_kernel(parts_ref, labels_ref, out_ref):
    total = parts_ref[0].astype(F32)
    for k in range(1, 8):
        total = total + parts_ref[k].astype(F32)
    squares = total[IMG : IMG + 1, 0:128] + total[IMG + 1 : IMG + 2, 0:128]
    scale = lax.rsqrt(squares / D + 1e-05)
    scale = jnp.where(labels_ref[3:4, 0:128].astype(F32) > 0.5, scale, 0.0)
    tile = jnp.broadcast_to(scale, (128, 128)).T[0:IMG]
    tile = jnp.concatenate([tile, tile], axis=1)
    out_ref[0:IMG, :] = jnp.where(tile > 0.0, total[0:IMG] * tile, 0.0).astype(BF)
    out_ref[IMG:, :] = labels_ref[...]


def close_images(parts, labels):
    return pl.pallas_call(
        close_kernel,
        out_shape=jax.ShapeDtypeStruct((IMG_TALL, 256), BF),
        cost_estimate=LIGHT,
        name="close_images",
    )(parts, labels)


def merge_kernel(
    place, slots, own_ref, rows_ref, first_ref, second_ref, near_ref, yonder_ref, side_ref, far_ref, out_ref, other
):
    prefill = place[0] == 0

    @pl.when(jnp.logical_and(prefill, pl.program_id(0) == 0))
    def _():
        other[...] = jnp.zeros_like(other)
        for p in range(PAGES):
            other[slots[p]] = rows_ref[p]

    def one(k):
        step = 2 * pl.program_id(0) + k
        match = jnp.where(prefill, step, place[3]).astype(F32)
        shard = jnp.where(prefill, place[3], step)
        level = lax.rem(place[3] - shard + 8, 4)
        close = (shard >= 4) == (place[3] >= 4)
        images = []
        for near, away in ((near_ref, yonder_ref), (side_ref, far_ref)):
            images.append(jnp.where(close, near[level], away[level]))
        targets = []
        for image in images:
            labels = image[IMG:IMG_TALL, 0:IMG].astype(F32)
            spot = labels[1:2] * PAGE + labels[2:3]
            targets.append(jnp.where(labels[0:1] == match, spot, -1.0))
        target = jnp.concatenate(targets, axis=1)
        data = jnp.concatenate([images[0][0:IMG], images[1][0:IMG]], axis=0)
        spots = lax.broadcasted_iota(jnp.int32, (CAP * PAGE, 2 * IMG), 0).astype(F32)
        chosen = (spots == target).astype(F32).astype(BF)
        image = jnp.dot(chosen, data, preferred_element_type=F32).astype(BF)

        def write(left, right):
            for half, text in enumerate((left, right)):
                lanes = slice(half * 128, half * 128 + 128)
                text = text.reshape(CAP * PAGE, 128)
                out_ref[k * CAP : (k + 1) * CAP, :, lanes] = (text + image[:, lanes]).reshape(CAP, PAGE, 128)

        @pl.when(prefill)
        def _():
            here = pl.ds(step * CAP, CAP)
            write(own_ref[0, k * CAP : (k + 1) * CAP], other[here])

        @pl.when(jnp.logical_not(prefill))
        def _():
            write(first_ref[0, k * CAP : (k + 1) * CAP], second_ref[0, k * CAP : (k + 1) * CAP])

    one(0)
    one(1)


def merge_slots(place, slots, own, rows, arrived, images):
    def local(i, place):
        return jnp.where(place[0] == 0, i, 3)

    def remote(i, place):
        return jnp.where(place[0] == 0, 0, i)

    image_spec = pl.BlockSpec((4, IMG_TALL, 256), lambda i, place, slots: (0, 0, 0))
    chunk = (1, 2 * CAP, PAGE, 128)
    return pl.pallas_call(
        merge_kernel,
        grid_spec=pltpu.PrefetchScalarGridSpec(
            num_scalar_prefetch=2,
            grid=(4,),
            in_specs=[
                pl.BlockSpec(chunk, lambda i, place, slots: (1, local(i, place), 0, 0)),
                pl.BlockSpec((PAGES, PAGE, 128), lambda i, place, slots: (0, 0, 0)),
                pl.BlockSpec(chunk, lambda i, place, slots: (0, remote(i, place), 0, 0)),
                pl.BlockSpec(chunk, lambda i, place, slots: (1, remote(i, place), 0, 0)),
            ]
            + [image_spec] * 4,
            out_specs=pl.BlockSpec((2 * CAP, PAGE, 256), lambda i, place, slots: (i, 0, 0)),
            scratch_shapes=[pltpu.VMEM((256, PAGE, 128), BF)],
        ),
        out_shape=jax.ShapeDtypeStruct((256, PAGE, 256), BF),
        compiler_params=pltpu.CompilerParams(vmem_limit_bytes=VMEM_LIMIT),
        cost_estimate=LIGHT,
        name="merge_slots",
    )(place, slots, own, rows, arrived, arrived, *images)


def attend(queries, kv_cache, new_kv, cache_lengths):
    row_count = queries.shape[0]
    heads_kv = kv_cache.shape[2] // (2 * HEAD)
    grouped = queries.reshape(row_count, heads_kv, queries.shape[1] // (HEAD * heads_kv), HEAD)
    stored = kv_cache.reshape(row_count, kv_cache.shape[1], heads_kv, 2 * HEAD)
    fresh_kv = new_kv.reshape(row_count, heads_kv, 2 * HEAD)
    scores = jnp.einsum(
        "rgqh,rjgh->rgqj", grouped, stored[..., :HEAD], preferred_element_type=jnp.float32
    ) * HEAD ** (-0.5)
    in_cache = jnp.arange(stored.shape[1], dtype=jnp.int32)[None, :] < cache_lengths[:, None]
    scores = jnp.where(in_cache[:, None, None, :], scores, -1e30)
    own_score = jnp.einsum(
        "rgqh,rgh->rgq", grouped, fresh_kv[..., :HEAD], preferred_element_type=jnp.float32
    ) * HEAD ** (-0.5)
    row_max = jnp.maximum(jnp.max(scores, axis=3), own_score)
    weights = jnp.exp(scores - row_max[..., None])
    own_weight = jnp.exp(own_score - row_max)
    denominator = jnp.sum(weights, axis=3) + own_weight
    probability = (weights / denominator[..., None]).astype(jnp.bfloat16)
    own_prob = lax.optimization_barrier((own_weight / denominator).astype(jnp.bfloat16)).astype(
        jnp.float32
    )
    attended = jnp.einsum(
        "rgqj,rjgh->rgqh", probability, stored[..., HEAD:], preferred_element_type=jnp.float32
    )
    attended = attended + own_prob[..., None] * fresh_kv[:, :, None, HEAD:].astype(jnp.float32)
    return attended.astype(jnp.bfloat16).reshape(row_count, queries.shape[1])


PARTNER = [(i, i ^ 1) for i in range(8)]


def shift(k):
    return [(i, (i + 2 * k) % 8) for i in range(8)]


def seq_shift(y, z):
    return [(i, (i // 4 + y) % 2 * 4 + (i + z) % 4) for i in range(8)]


FAR = [(g * 8 + i, (1 - g) * 8 + (i + 4) % 8) for g in range(2) for i in range(8)]


def after(value, other):
    return lax.optimization_barrier((value, other))[0]


def per_device(
    embeds,
    image_feats,
    image_pos,
    proj_w,
    proj_b,
    norm_gain,
    kv_w,
    prompt_lengths,
    page_owner,
    queries,
    kv_cache,
    new_kv,
    cache_lengths,
):
    group = lax.axis_index("group").astype(jnp.int32)
    seq = lax.axis_index("seq").astype(jnp.int32)
    mp = lax.axis_index("mp").astype(jnp.int32)
    core, x = mp % 2, mp // 2
    place = jnp.stack([group, core, x, seq])


    owners = page_owner[:, 0]
    before = (
        jnp.arange(PAGES, dtype=jnp.int32)[None, :] < jnp.arange(PAGES, dtype=jnp.int32)[:, None]
    )
    page_rank = jnp.sum((before & (owners[:, None] == owners[None, :])).astype(jnp.int32), axis=1)
    slots = owners * CAP + page_rank
    live = jnp.sum(jnp.where(jnp.arange(4, dtype=jnp.int32) == seq // 2, prompt_lengths, 0))
    limit = live - (seq % 2) * ROWS
    local_pos = lax.dynamic_slice(image_pos, (group * IMG,), (IMG,)) - seq * ROWS
    at_page = (local_pos // PAGE)[:, None] == jnp.arange(PAGES, dtype=jnp.int32)[None, :]
    image_owner = jnp.sum(jnp.where(at_page, owners[None, :], 0), axis=1)
    image_rank = jnp.sum(jnp.where(at_page, page_rank[None, :], 0), axis=1)
    labels = jnp.stack(
        [image_owner, image_rank, local_pos % PAGE, (local_pos < limit).astype(jnp.int32)]
    ).astype(BF)
    tokens = jnp.arange(ROWS, dtype=jnp.int32).reshape(16, 128)
    places = image_pos - seq * ROWS
    upper = (places // 128)[None, :] == jnp.arange(16, dtype=jnp.int32)[:, None]
    lower = (places % 128)[:, None] == jnp.arange(128, dtype=jnp.int32)[None, :]
    is_image = jnp.dot(upper.astype(BF), lower.astype(BF), preferred_element_type=F32)
    mask = jnp.where((tokens < limit) & (is_image < 0.5), 1.0, 0.0).astype(F32)
    labels = jnp.pad(labels, ((0, 12), (0, 256 - IMG)))

    got = lax.all_to_all(cut_features(place, image_feats), "seq", 0, 0, tiled=True)

    send, keep = project_text(place, embeds, norm_gain, kv_w)
    got = after(got, keep[0])
    swapped = lax.ppermute(got, "mp", PARTNER)
    received = [lax.ppermute(piece, "mp", PARTNER) for piece in send]

    feats = jnp.concatenate([got, swapped], axis=1).reshape(8 * IMG, -1)
    partial = jnp.dot(feats, proj_w, preferred_element_type=F32).astype(BF).reshape(8, IMG, -1)
    pieces = lax.all_to_all(partial, "seq", 0, 0, tiled=True)

    added = [None] + [add_pair(after(keep[j], partial), received[j]) for j in (1, 2, 3)]
    base = keep[0].astype(F32) + after(received[0], added[1:]).astype(F32)
    parts = [base] + [lax.ppermute(added[j], "mp", shift(j)) for j in (1, 2, 3)]

    image_hidden, heads = image_rows_kv(
        place, after(pieces, base), proj_b, norm_gain, kv_w
    )
    image_parts = lax.all_to_all(heads, "mp", 0, 0, tiled=True)
    image_block = close_images(image_parts, labels)

    rows, by_owner = finish_text(slots, after(mask, image_block), parts)
    other_rows = lax.ppermute(rows, "group", [(1, 0)])
    arrived = lax.all_to_all(
        by_owner.reshape(512, PAGE, 128), ("group", "seq"), split_axis=0, concat_axis=0, tiled=True
    ).reshape(2, 256, PAGE, 128)

    near = jnp.stack(
        [image_block] + [lax.ppermute(image_block, "seq", seq_shift(0, k)) for k in (1, 2, 3)]
    )
    images = [
        near,
        lax.ppermute(near, "seq", seq_shift(1, 0)),
        lax.ppermute(near, "group", [(0, 1), (1, 0)]),
        lax.ppermute(near, ("group", "seq"), FAR),
    ]
    attended = lax.cond(
        group != 0,
        attend,
        lambda *unused: jnp.zeros(queries.shape, BF),
        after(queries, near),
        kv_cache,
        new_kv,
        cache_lengths,
    )
    page_slots = merge_slots(place, slots, by_owner, other_rows, arrived, images)

    other_hidden = lax.ppermute(image_hidden, "group", [(1, 0)])
    row_states = jnp.where(
        group == 0, jnp.concatenate([image_hidden, other_hidden], axis=0), attended
    )
    return (page_slots, row_states)


def solution(mesh):
    in_specs = (
        P("seq", "mp"),
        P("seq", None),
        P("seq"),
        P("seq", "mp"),
        P("mp"),
        P("mp"),
        P("mp", None),
        P(),
        P("seq", None),
        P("seq", "mp"),
        P("seq", None, "mp"),
        P("seq", "mp"),
        P("seq"),
    )
    out_specs = (P(("group", "seq"), None, "mp"), P(("group", "seq"), "mp"))
    return jax.shard_map(
        per_device, mesh=mesh, in_specs=in_specs, out_specs=out_specs, check_vma=False
    )
```

```python
import functools

import jax
import jax.numpy as jnp
from jax import lax
from jax.experimental import pallas as pl
from jax.experimental.pallas import tpu as pltpu
from jax.sharding import PartitionSpec as P

D = 8192
HEAD = 128
PAGE = 16
PROMPT_LEN = 4096
CAP = 32
ROWS = 2048
EXT = 32
TALL = ROWS + EXT
PAGES = ROWS // PAGE
IMG = 64
IMG_TALL = IMG + 16
BF = jnp.bfloat16
F32 = jnp.float32
def work(micros):
    size = int(micros * 3700000)
    return pl.CostEstimate(flops=micros * 1000000, bytes_accessed=size, transcendentals=0)


LIGHT = pl.CostEstimate(flops=1, bytes_accessed=1, transcendentals=0)
VMEM_LIMIT = 56 * 1024 * 1024


def split_pair(value):
    high = value.astype(BF)
    low = (value - high.astype(F32)).astype(BF)
    return high, low


TILE = 512
STEPS = ROWS // TILE


def project_kernel(place, embeds_ref, gain_ref, *refs):
    weights, send, keep, squares_ref = refs[0:8], refs[8:12], refs[12:16], refs[16]
    step = pl.program_id(0)

    @pl.when(step < STEPS)
    def _():
        hidden = embeds_ref[...].astype(F32)
        scaled = (hidden * gain_ref[...].astype(F32).reshape(1, -1)).astype(BF)
        squared = hidden * hidden
        lanes = squared[:, 0:128]
        for k in range(1, 8):
            lanes = lanes + squared[:, k * 128 : (k + 1) * 128]
        summed = jnp.sum(lanes.T, axis=0, keepdims=True)
        for k in range(TILE // 128):
            squares_ref[pl.ds(TILE // 128 * step + k, 1), :] = summed[:, k * 128 : (k + 1) * 128]
        for k, target in enumerate((send[:2], send[2:], keep[:2], keep[2:])):
            weight = jnp.concatenate([weights[2 * k][...], weights[2 * k + 1][...]], axis=1)
            product = jnp.dot(scaled, weight, preferred_element_type=F32).astype(BF)
            target[0][...] = product[:, :128]
            target[1][...] = product[:, 128:]

    @pl.when(step == STEPS)
    def _():
        high, low = split_pair(squares_ref[...])
        both = jnp.concatenate([high, low], axis=0)
        for ref in (*send, *keep):
            ref[0:EXT, :] = both


def project_text(place, embeds, gain, kv_w):
    def column(r, j):
        def index(i, place):
            core = place[1] if r else 1 - place[1]
            head = 2 * lax.rem(place[2] + j, 4) + core
            return (0, 2 * head + place[0])

        return index

    specs = [
        pl.BlockSpec((TILE, 1024), lambda i, place: (jnp.minimum(i, STEPS - 1), 0)),
        pl.BlockSpec((1024,), lambda i, place: (0,)),
    ] + [pl.BlockSpec((1024, 128), column(r, j)) for r in range(2) for j in range(4)]
    outs = pl.pallas_call(
        project_kernel,
        grid_spec=pltpu.PrefetchScalarGridSpec(
            num_scalar_prefetch=1,
            grid=(STEPS + 1,),
            in_specs=specs,
            out_specs=[pl.BlockSpec((TILE, 128), lambda i, place: (i, 0))] * 8,
            scratch_shapes=[pltpu.VMEM((16, 128), F32)],
        ),
        out_shape=[jax.ShapeDtypeStruct((TALL, 128), BF)] * 8,
        compiler_params=pltpu.CompilerParams(vmem_limit_bytes=VMEM_LIMIT),
        cost_estimate=LIGHT,
        name="project_text",
    )(place, embeds, gain, *([kv_w] * 8))
    return outs[:4], outs[4:]


def square_rows(refs):
    total = jnp.zeros((16, 128), F32)
    for ref in refs:
        total = total + ref[ROWS : ROWS + 16, :].astype(F32) + ref[ROWS + 16 : TALL, :].astype(F32)
    return total


def add_pair(keep, received):
    return (keep.astype(F32) + received.astype(F32)).astype(BF)


def finish_kernel(slots, mask_ref, *refs):
    parts, rows_ref, stack_ref, moved = refs[:4], refs[4], refs[5], refs[6:]
    stack_ref[...] = jnp.zeros_like(stack_ref)
    squares = square_rows(parts)
    scale = jnp.where(mask_ref[...] > 0.0, lax.rsqrt(squares / D + 1e-05), 0.0)
    for part in range(16):
        tile = jnp.broadcast_to(scale[part : part + 1, :], (128, 128)).T
        here = slice(part * 128, part * 128 + 128)
        total = parts[0][here, :].astype(F32)
        for ref in parts[1:]:
            total = total + ref[here, :].astype(F32)
        rows = jnp.where(tile > 0.0, total * tile, 0.0).astype(BF)
        for p in range(8):
            page = rows[p * PAGE : (p + 1) * PAGE, :]
            rows_ref[part * 8 + p] = page
            stack_ref[slots[part * 8 + p]] = page
    for k, ref in enumerate(moved):
        ref[...] = stack_ref[64 * (k + 1) : 64 * (k + 2)]


def finish_text(slots, mask, parts):
    whole = lambda i, slots: (0, 0)
    return pl.pallas_call(
        finish_kernel,
        grid_spec=pltpu.PrefetchScalarGridSpec(
            num_scalar_prefetch=1,
            grid=(1,),
            in_specs=[pl.BlockSpec((16, 128), whole)] + [pl.BlockSpec((TALL, 128), whole)] * 4,
            out_specs=[
                pl.BlockSpec((count, PAGE, 128), lambda i, slots: (0, 0, 0))
                for count in (PAGES, 256, 64, 64, 64)
            ],
        ),
        out_shape=[
            jax.ShapeDtypeStruct((count, PAGE, 128), BF) for count in (PAGES, 256, 64, 64, 64)
        ],
        compiler_params=pltpu.CompilerParams(vmem_limit_bytes=VMEM_LIMIT),
        cost_estimate=work(20000),
        name="finish_text",
    )(slots, mask, *parts)


def cut_kernel(place, feats_ref, out_ref):
    depth = out_ref.shape[2]
    for k in range(8):
        out_ref[k] = feats_ref[:, k * depth : (k + 1) * depth]


def cut_features(place, feats):
    depth = feats.shape[1] // 8
    return pl.pallas_call(
        cut_kernel,
        grid_spec=pltpu.PrefetchScalarGridSpec(
            num_scalar_prefetch=1,
            grid=(1,),
            in_specs=[
                pl.BlockSpec((32, feats.shape[1]), lambda i, place: (2 * place[0] + place[1], 0))
            ],
            out_specs=pl.BlockSpec((8, 32, depth), lambda i, place: (0, 0, 0)),
        ),
        out_shape=jax.ShapeDtypeStruct((8, 32, depth), BF),
        cost_estimate=LIGHT,
        name="cut_features",
    )(place, feats)


def image_kernel(
    place, pieces_ref, bias_ref, gain_ref, weight_ref, hidden_ref, heads_ref, scaled, pair
):
    step = pl.program_id(0)

    @pl.when(step == 0)
    def _():
        total = pieces_ref[0].astype(F32)
        for k in range(1, 8):
            total = total + pieces_ref[k].astype(F32)
        flipped = jnp.concatenate([total[32:64], total[0:32]], axis=0)
        total = jnp.where(place[1] == 0, total, flipped)
        total = total + bias_ref[...].astype(F32).reshape(1, -1)
        image_hidden = (0.5 * total * (1.0 + lax.erf(total * (0.5**0.5)))).astype(BF)
        hidden_ref[...] = image_hidden
        hidden = image_hidden.astype(F32)
        scaled[...] = (hidden * gain_ref[...].astype(F32).reshape(1, -1)).astype(BF)
        squared = hidden * hidden
        lanes = squared[:, 0:128]
        for k in range(1, 8):
            lanes = lanes + squared[:, k * 128 : (k + 1) * 128]
        lanes = jnp.concatenate([lanes, jnp.zeros_like(lanes)], axis=0)
        summed = jnp.sum(lanes.T, axis=0, keepdims=True)
        high, low = split_pair(summed)
        picked = lax.broadcasted_iota(jnp.int32, (16, 128), 0)
        rows = jnp.where(picked == 0, high.astype(F32), jnp.where(picked == 1, low.astype(F32), 0.0))
        pair[...] = jnp.concatenate([rows, jnp.zeros_like(rows)], axis=1).astype(BF)

    product = jnp.dot(scaled[...], weight_ref[...], preferred_element_type=F32)
    for k in range(2):
        heads_ref[k, 0:IMG, :] = product[:, 256 * k : 256 * (k + 1)].astype(BF)
        heads_ref[k, IMG:, :] = pair[...]


def image_rows_kv(place, pieces, bias, gain, kv_w):
    width = pieces.shape[2]
    row = pl.BlockSpec((width,), lambda i, place: (0,))
    return pl.pallas_call(
        image_kernel,
        grid_spec=pltpu.PrefetchScalarGridSpec(
            num_scalar_prefetch=1,
            grid=(4,),
            in_specs=[
                pl.BlockSpec((8, IMG, width), lambda i, place: (0, 0, 0)),
                row,
                row,
                pl.BlockSpec((width, 512), lambda i, place: (0, i)),
            ],
            out_specs=[
                pl.BlockSpec((IMG, width), lambda i, place: (0, 0)),
                pl.BlockSpec((2, IMG_TALL, 256), lambda i, place: (i, 0, 0)),
            ],
            scratch_shapes=[pltpu.VMEM((IMG, width), BF), pltpu.VMEM((16, 256), BF)],
        ),
        out_shape=[
            jax.ShapeDtypeStruct((IMG, width), BF),
            jax.ShapeDtypeStruct((8, IMG_TALL, 256), BF),
        ],
        compiler_params=pltpu.CompilerParams(vmem_limit_bytes=VMEM_LIMIT),
        cost_estimate=LIGHT,
        name="image_rows_kv",
    )(place, pieces, bias, gain, kv_w)


def close_kernel(parts_ref, labels_ref, out_ref):
    total = parts_ref[0].astype(F32)
    for k in range(1, 8):
        total = total + parts_ref[k].astype(F32)
    squares = total[IMG : IMG + 1, 0:128] + total[IMG + 1 : IMG + 2, 0:128]
    scale = lax.rsqrt(squares / D + 1e-05)
    scale = jnp.where(labels_ref[3:4, 0:128].astype(F32) > 0.5, scale, 0.0)
    tile = jnp.broadcast_to(scale, (128, 128)).T[0:IMG]
    tile = jnp.concatenate([tile, tile], axis=1)
    rows = jnp.where(tile > 0.0, total[0:IMG] * tile, 0.0).astype(BF)
    block = jnp.concatenate([rows, labels_ref[...]], axis=0)
    out_ref[...] = block


def close_images(parts, labels):
    return pl.pallas_call(
        close_kernel,
        out_shape=jax.ShapeDtypeStruct((IMG_TALL, 256), BF),
        cost_estimate=LIGHT,
        name="close_images",
    )(parts, labels)


def merge_kernel(
    place,
    slots,
    own_ref,
    rows_ref,
    next_ref,
    cross_ref,
    stay_ref,
    other_ref,
    image0,
    image1,
    image2,
    image3,
    out_ref,
    placed,
):
    prefill = place[0] == 0
    step = pl.program_id(0)
    here, there = place[3] // 4, 1 - place[3] // 4

    @pl.when(jnp.logical_and(prefill, step == 0))
    def _():
        placed[...] = jnp.zeros_like(placed)
        for p in range(PAGES):
            placed[slots[p]] = rows_ref[p]

    spots = lax.broadcasted_iota(jnp.int32, (CAP * PAGE, 2 * IMG), 0).astype(F32)

    def one(images, owner, upper, left, right):
        targets = []
        for image in images:
            labels = image[0, IMG:IMG_TALL, 0:IMG].astype(F32)
            spot = labels[1:2] * PAGE + labels[2:3]
            targets.append(jnp.where(labels[0:1] == owner.astype(F32), spot, -1.0))
        target = jnp.concatenate(targets, axis=1)
        data = jnp.concatenate([images[0][0, 0:IMG, :], images[1][0, 0:IMG, :]], axis=0)
        chosen = (spots == target).astype(F32).astype(BF)
        image = jnp.dot(chosen, data, preferred_element_type=F32).astype(BF)
        for half, text in enumerate((left, right)):
            lanes = slice(half * 128, half * 128 + 128)
            merged = text.reshape(CAP * PAGE, 128) + image[:, lanes]
            out_ref[upper, 0, :, :, lanes] = merged.reshape(CAP, PAGE, 128)

    @pl.when(prefill)
    def _():
        level = lax.rem(place[3] + step, 4)
        for k, upper in enumerate((here, there)):
            start = (2 * step + k) * CAP
            one((image0, image1), upper * 4 + level, upper, own_ref[k], placed[pl.ds(start, CAP)])

    @pl.when(jnp.logical_not(prefill))
    def _():
        one((image0, image1), place[3], here, next_ref[0], stay_ref[0])
        one((image2, image3), place[3], there, cross_ref[0], other_ref[0])


def merge_slots(place, slots, stack, rows, blocks, images):
    def level(i, place):
        return lax.rem(jnp.where(place[0] == 0, place[3] + i, place[3] + 8 - i), 4)

    def image_spec(apart):
        def index(i, place, slots):
            y = place[3] // 4
            y = 1 - y if apart else y
            return (jnp.where(place[0] == 0, place[3], 4 * y + level(i, place)), 0, 0)

        return pl.BlockSpec((1, IMG_TALL, 256), index)

    def local(i, place, slots):
        return (jnp.where(place[0] == 0, i, 0), 0, 0, 0)

    def remote(i, place, slots):
        return (jnp.where(place[0] == 0, 0, i), 0, 0, 0)

    chunk = pl.BlockSpec((1, CAP, PAGE, 128), remote)
    result = pl.pallas_call(
        merge_kernel,
        grid_spec=pltpu.PrefetchScalarGridSpec(
            num_scalar_prefetch=2,
            grid=(4,),
            in_specs=[
                pl.BlockSpec((2, CAP, PAGE, 128), local),
                pl.BlockSpec((PAGES, PAGE, 128), lambda i, place, slots: (0, 0, 0)),
                chunk,
                chunk,
                chunk,
                chunk,
                image_spec(False),
                image_spec(False),
                image_spec(True),
                image_spec(True),
            ],
            out_specs=pl.BlockSpec(
                (2, 1, CAP, PAGE, 256), lambda i, place, slots: (0, level(i, place), 0, 0, 0)
            ),
            scratch_shapes=[pltpu.VMEM((256, PAGE, 128), BF)],
        ),
        out_shape=jax.ShapeDtypeStruct((2, 4, CAP, PAGE, 256), BF),
        compiler_params=pltpu.CompilerParams(vmem_limit_bytes=VMEM_LIMIT),
        cost_estimate=LIGHT,
        name="merge_slots",
    )(place, slots, stack.reshape(8, CAP, PAGE, 128), rows, *blocks, *images, *images)
    return result.reshape(256, PAGE, 256)


def attend(queries, kv_cache, new_kv, cache_lengths):
    row_count = queries.shape[0]
    heads_kv = kv_cache.shape[2] // (2 * HEAD)
    grouped = queries.reshape(row_count, heads_kv, queries.shape[1] // (HEAD * heads_kv), HEAD)
    stored = kv_cache.reshape(row_count, kv_cache.shape[1], heads_kv, 2 * HEAD)
    fresh_kv = new_kv.reshape(row_count, heads_kv, 2 * HEAD)
    scores = jnp.einsum(
        "rgqh,rjgh->rgqj", grouped, stored[..., :HEAD], preferred_element_type=jnp.float32
    ) * HEAD ** (-0.5)
    in_cache = jnp.arange(stored.shape[1], dtype=jnp.int32)[None, :] < cache_lengths[:, None]
    scores = jnp.where(in_cache[:, None, None, :], scores, -1e30)
    own_score = jnp.einsum(
        "rgqh,rgh->rgq", grouped, fresh_kv[..., :HEAD], preferred_element_type=jnp.float32
    ) * HEAD ** (-0.5)
    row_max = jnp.maximum(jnp.max(scores, axis=3), own_score)
    weights = jnp.exp(scores - row_max[..., None])
    own_weight = jnp.exp(own_score - row_max)
    denominator = jnp.sum(weights, axis=3) + own_weight
    probability = (weights / denominator[..., None]).astype(jnp.bfloat16)
    own_prob = lax.optimization_barrier((own_weight / denominator).astype(jnp.bfloat16)).astype(
        jnp.float32
    )
    attended = jnp.einsum(
        "rgqj,rjgh->rgqh", probability, stored[..., HEAD:], preferred_element_type=jnp.float32
    )
    attended = attended + own_prob[..., None] * fresh_kv[:, :, None, HEAD:].astype(jnp.float32)
    return attended.astype(jnp.bfloat16).reshape(row_count, queries.shape[1])


PARTNER = [(i, i ^ 1) for i in range(8)]


def shift(k):
    return [(i, (i + 2 * k) % 8) for i in range(8)]


def seq_shift(y, z):
    return [(i, (i // 4 + y) % 2 * 4 + (i + z) % 4) for i in range(8)]


CROSS = [(i, 8 + (i + 4) % 8) for i in range(8)]
AWAY = [(8 + i, 8 + (i + 4) % 8) for i in range(8)]


def after(value, other):
    return lax.optimization_barrier((value, other))[0]


def per_device(
    embeds,
    image_feats,
    image_pos,
    proj_w,
    proj_b,
    norm_gain,
    kv_w,
    prompt_lengths,
    page_owner,
    queries,
    kv_cache,
    new_kv,
    cache_lengths,
):
    group = lax.axis_index("group").astype(jnp.int32)
    seq = lax.axis_index("seq").astype(jnp.int32)
    mp = lax.axis_index("mp").astype(jnp.int32)
    core, x = mp % 2, mp // 2
    place = jnp.stack([group, core, x, seq])


    owners = page_owner[:, 0]
    before = (
        jnp.arange(PAGES, dtype=jnp.int32)[None, :] < jnp.arange(PAGES, dtype=jnp.int32)[:, None]
    )
    page_rank = jnp.sum((before & (owners[:, None] == owners[None, :])).astype(jnp.int32), axis=1)
    distance = 2 * ((owners % 4 - seq % 4) % 4) + (owners // 4 != seq // 4).astype(jnp.int32)
    slots = distance * CAP + page_rank
    live = jnp.sum(jnp.where(jnp.arange(4, dtype=jnp.int32) == seq // 2, prompt_lengths, 0))
    limit = live - (seq % 2) * ROWS
    local_pos = lax.dynamic_slice(image_pos, (group * IMG,), (IMG,)) - seq * ROWS
    at_page = (local_pos // PAGE)[:, None] == jnp.arange(PAGES, dtype=jnp.int32)[None, :]
    image_owner = jnp.sum(jnp.where(at_page, owners[None, :], 0), axis=1)
    image_rank = jnp.sum(jnp.where(at_page, page_rank[None, :], 0), axis=1)
    labels = jnp.stack(
        [image_owner, image_rank, local_pos % PAGE, (local_pos < limit).astype(jnp.int32)]
    ).astype(BF)
    tokens = jnp.arange(ROWS, dtype=jnp.int32).reshape(16, 128)
    places = image_pos - seq * ROWS
    upper = (places // 128)[None, :] == jnp.arange(16, dtype=jnp.int32)[:, None]
    lower = (places % 128)[:, None] == jnp.arange(128, dtype=jnp.int32)[None, :]
    is_image = jnp.dot(upper.astype(BF), lower.astype(BF), preferred_element_type=F32)
    mask = jnp.where((tokens < limit) & (is_image < 0.5), 1.0, 0.0).astype(F32)
    labels = jnp.pad(labels, ((0, 12), (0, 256 - IMG)))

    got = lax.all_to_all(cut_features(place, image_feats), "seq", 0, 0, tiled=True)

    send, keep = project_text(place, embeds, norm_gain, kv_w)
    got = after(got, keep[0])
    swapped = lax.ppermute(got, "mp", PARTNER)
    received = [lax.ppermute(piece, "mp", PARTNER) for piece in send]

    added = [None] + [add_pair(keep[j], received[j]) for j in (1, 2, 3)]
    base = keep[0].astype(F32) + after(received[0], added[1:]).astype(F32)
    parts = [base] + [lax.ppermute(added[j], "mp", shift(j)) for j in (1, 2, 3)]

    feats = jnp.concatenate([got, after(swapped, base)], axis=1).reshape(8 * IMG, -1)
    partial = jnp.dot(feats, proj_w, preferred_element_type=F32).astype(BF).reshape(8, IMG, -1)
    pieces = lax.all_to_all(partial, "seq", 0, 0, tiled=True)

    attended = lax.cond(
        group != 0,
        attend,
        lambda *unused: jnp.zeros(queries.shape, BF),
        after(queries, partial),
        kv_cache,
        new_kv,
        cache_lengths,
    )
    rows, stack, *moved = finish_text(slots, after(mask, attended), parts)
    image_hidden, heads = image_rows_kv(place, after(pieces, stack), proj_b, norm_gain, kv_w)
    levels = [stack[:64]] + [
        lax.ppermute(moved[k - 1], "seq", seq_shift(0, k)) for k in (1, 2, 3)
    ]
    levels = [piece.reshape(2, CAP, PAGE, 128) for piece in after(levels, heads)]
    stay = jnp.stack([piece[0] for piece in levels])
    leave = jnp.stack([piece[1] for piece in levels])
    neighbour = lax.ppermute(stay, "group", [(0, 1)])
    cross = lax.ppermute(leave, ("group", "seq"), CROSS)
    away = lax.ppermute(leave, ("group", "seq"), AWAY)
    other_rows = lax.ppermute(rows, "group", [(1, 0)])

    image_parts = lax.all_to_all(heads, "mp", 0, 0, tiled=True)
    image_copies = close_images(after(image_parts, (stay, leave)), labels)
    images = lax.all_gather(image_copies, "seq", axis=0)
    other_images = lax.ppermute(images, "group", [(0, 1), (1, 0)])
    other_hidden = lax.ppermute(image_hidden, "group", [(1, 0)])

    page_slots = merge_slots(place, slots, stack, other_rows, (neighbour, cross, stay, away), (images, other_images))

    row_states = jnp.where(
        group == 0, jnp.concatenate([image_hidden, other_hidden], axis=0), attended
    )
    return (page_slots, row_states)


def solution(mesh):
    in_specs = (
        P("seq", "mp"),
        P("seq", None),
        P("seq"),
        P("seq", "mp"),
        P("mp"),
        P("mp"),
        P("mp", None),
        P(),
        P("seq", None),
        P("seq", "mp"),
        P("seq", None, "mp"),
        P("seq", "mp"),
        P("seq"),
    )
    out_specs = (P(("group", "seq"), None, "mp"), P(("group", "seq"), "mp"))
    return jax.shard_map(
        per_device, mesh=mesh, in_specs=in_specs, out_specs=out_specs, check_vma=False
    )
```

```python
import functools

import jax
import jax.numpy as jnp
from jax import lax
from jax.experimental import pallas as pl
from jax.experimental.pallas import tpu as pltpu
from jax.sharding import PartitionSpec as P

D = 8192
HEAD = 128
PAGE = 16
PROMPT_LEN = 4096
CAP = 32
ROWS = 2048
EXT = 32
TALL = ROWS + EXT
PAGES = ROWS // PAGE
IMG = 64
IMG_TALL = IMG + 16
BF = jnp.bfloat16
F32 = jnp.float32
def work(micros):
    size = int(micros * 3700000)
    return pl.CostEstimate(flops=micros * 1000000, bytes_accessed=size, transcendentals=0)


LIGHT = pl.CostEstimate(flops=1, bytes_accessed=1, transcendentals=0)
VMEM_LIMIT = 56 * 1024 * 1024


def split_pair(value):
    high = value.astype(BF)
    low = (value - high.astype(F32)).astype(BF)
    return high, low


TILE = 512
STEPS = ROWS // TILE


def project_kernel(place, embeds_ref, gain_ref, *refs):
    weights, send, keep, squares_ref = refs[0:8], refs[8:12], refs[12:16], refs[16]
    step = pl.program_id(0)

    @pl.when(step < STEPS)
    def _():
        hidden = embeds_ref[...].astype(F32)
        scaled = (hidden * gain_ref[...].astype(F32).reshape(1, -1)).astype(BF)
        squared = hidden * hidden
        lanes = squared[:, 0:128]
        for k in range(1, 8):
            lanes = lanes + squared[:, k * 128 : (k + 1) * 128]
        summed = jnp.sum(lanes.T, axis=0, keepdims=True)
        for k in range(TILE // 128):
            squares_ref[pl.ds(TILE // 128 * step + k, 1), :] = summed[:, k * 128 : (k + 1) * 128]
        for k, target in enumerate((send[:2], send[2:], keep[:2], keep[2:])):
            weight = jnp.concatenate([weights[2 * k][...], weights[2 * k + 1][...]], axis=1)
            product = jnp.dot(scaled, weight, preferred_element_type=F32).astype(BF)
            target[0][...] = product[:, :128]
            target[1][...] = product[:, 128:]

    @pl.when(step == STEPS)
    def _():
        high, low = split_pair(squares_ref[...])
        both = jnp.concatenate([high, low], axis=0)
        for ref in (*send, *keep):
            ref[0:EXT, :] = both


def project_text(place, embeds, gain, kv_w):
    def column(r, j):
        def index(i, place):
            core = place[1] if r else 1 - place[1]
            head = 2 * lax.rem(place[2] + j, 4) + core
            return (0, 2 * head + place[0])

        return index

    specs = [
        pl.BlockSpec((TILE, 1024), lambda i, place: (jnp.minimum(i, STEPS - 1), 0)),
        pl.BlockSpec((1024,), lambda i, place: (0,)),
    ] + [pl.BlockSpec((1024, 128), column(r, j)) for r in range(2) for j in range(4)]
    outs = pl.pallas_call(
        project_kernel,
        grid_spec=pltpu.PrefetchScalarGridSpec(
            num_scalar_prefetch=1,
            grid=(STEPS + 1,),
            in_specs=specs,
            out_specs=[pl.BlockSpec((TILE, 128), lambda i, place: (i, 0))] * 8,
            scratch_shapes=[pltpu.VMEM((16, 128), F32)],
        ),
        out_shape=[jax.ShapeDtypeStruct((TALL, 128), BF)] * 8,
        compiler_params=pltpu.CompilerParams(vmem_limit_bytes=VMEM_LIMIT),
        cost_estimate=LIGHT,
        name="project_text",
    )(place, embeds, gain, *([kv_w] * 8))
    return outs[:4], outs[4:]


def square_rows(refs):
    total = jnp.zeros((16, 128), F32)
    for ref in refs:
        total = total + ref[ROWS : ROWS + 16, :].astype(F32) + ref[ROWS + 16 : TALL, :].astype(F32)
    return total


def add_pair(keep, received):
    return (keep.astype(F32) + received.astype(F32)).astype(BF)


def finish_kernel(slots, mask_ref, *refs):
    parts, (rows_ref, slot_ref) = refs[:5], refs[5:]
    slot_ref[...] = jnp.zeros_like(slot_ref)
    squares = square_rows(parts)
    scale = jnp.where(mask_ref[...] > 0.0, lax.rsqrt(squares / D + 1e-05), 0.0)
    for part in range(16):
        tile = jnp.broadcast_to(scale[part : part + 1, :], (128, 128)).T
        here = slice(part * 128, part * 128 + 128)
        total = parts[0][here, :].astype(F32)
        for ref in parts[1:]:
            total = total + ref[here, :].astype(F32)
        rows = jnp.where(tile > 0.0, total * tile, 0.0).astype(BF)
        for p in range(8):
            page = rows[p * PAGE : (p + 1) * PAGE, :]
            rows_ref[part * 8 + p] = page
            slot_ref[0, slots[part * 8 + p]] = page


def finish_text(slots, mask, parts):
    whole = lambda i, slots: (0, 0)
    return pl.pallas_call(
        finish_kernel,
        grid_spec=pltpu.PrefetchScalarGridSpec(
            num_scalar_prefetch=1,
            grid=(1,),
            in_specs=[pl.BlockSpec((16, 128), whole)] + [pl.BlockSpec((TALL, 128), whole)] * 5,
            out_specs=[
                pl.BlockSpec((PAGES, PAGE, 128), lambda i, slots: (0, 0, 0)),
                pl.BlockSpec((1, 256, PAGE, 128), lambda i, slots: (1, 0, 0, 0)),
            ],
        ),
        out_shape=[
            jax.ShapeDtypeStruct((PAGES, PAGE, 128), BF),
            jax.ShapeDtypeStruct((2, 256, PAGE, 128), BF),
        ],
        compiler_params=pltpu.CompilerParams(vmem_limit_bytes=VMEM_LIMIT),
        cost_estimate=work(20000),
        name="finish_text",
    )(slots, mask, *parts)


def cut_kernel(place, feats_ref, out_ref):
    depth = out_ref.shape[2]
    for k in range(8):
        out_ref[k] = feats_ref[:, k * depth : (k + 1) * depth]


def cut_features(place, feats):
    depth = feats.shape[1] // 8
    return pl.pallas_call(
        cut_kernel,
        grid_spec=pltpu.PrefetchScalarGridSpec(
            num_scalar_prefetch=1,
            grid=(1,),
            in_specs=[
                pl.BlockSpec((32, feats.shape[1]), lambda i, place: (2 * place[0] + place[1], 0))
            ],
            out_specs=pl.BlockSpec((8, 32, depth), lambda i, place: (0, 0, 0)),
        ),
        out_shape=jax.ShapeDtypeStruct((8, 32, depth), BF),
        cost_estimate=LIGHT,
        name="cut_features",
    )(place, feats)


def image_kernel(
    place, pieces_ref, bias_ref, gain_ref, weight_ref, hidden_ref, swap_ref, same_ref, scaled, pair
):
    step = pl.program_id(0)

    @pl.when(step == 0)
    def _():
        total = pieces_ref[0].astype(F32)
        for k in range(1, 8):
            total = total + pieces_ref[k].astype(F32)
        flipped = jnp.concatenate([total[32:64], total[0:32]], axis=0)
        total = jnp.where(place[1] == 0, total, flipped)
        total = total + bias_ref[...].astype(F32).reshape(1, -1)
        image_hidden = (0.5 * total * (1.0 + lax.erf(total * (0.5**0.5)))).astype(BF)
        hidden_ref[...] = image_hidden
        hidden = image_hidden.astype(F32)
        scaled[...] = (hidden * gain_ref[...].astype(F32).reshape(1, -1)).astype(BF)
        squared = hidden * hidden
        lanes = squared[:, 0:128]
        for k in range(1, 8):
            lanes = lanes + squared[:, k * 128 : (k + 1) * 128]
        lanes = jnp.concatenate([lanes, jnp.zeros_like(lanes)], axis=0)
        summed = jnp.sum(lanes.T, axis=0, keepdims=True)
        high, low = split_pair(summed)
        picked = lax.broadcasted_iota(jnp.int32, (16, 128), 0)
        rows = jnp.where(picked == 0, high.astype(F32), jnp.where(picked == 1, low.astype(F32), 0.0))
        pair[...] = jnp.concatenate([rows, jnp.zeros_like(rows)], axis=1).astype(BF)

    product = jnp.dot(scaled[...], weight_ref[...], preferred_element_type=F32)
    left, right = product[:, :256], product[:, 256:]
    first = place[1] == 0
    same_ref[0, 0:IMG, :] = jnp.where(first, left, right).astype(BF)
    swap_ref[0, 0:IMG, :] = jnp.where(first, right, left).astype(BF)
    same_ref[0, IMG:, :] = pair[...]
    swap_ref[0, IMG:, :] = pair[...]


def image_rows_kv(place, pieces, bias, gain, kv_w):
    def column(i, place):
        return (0, lax.rem(place[2] + i, 4))

    width = pieces.shape[2]
    row = pl.BlockSpec((width,), lambda i, place: (0,))
    out = jax.ShapeDtypeStruct((4, IMG_TALL, 256), BF)
    return pl.pallas_call(
        image_kernel,
        grid_spec=pltpu.PrefetchScalarGridSpec(
            num_scalar_prefetch=1,
            grid=(4,),
            in_specs=[
                pl.BlockSpec((8, IMG, width), lambda i, place: (0, 0, 0)),
                row,
                row,
                pl.BlockSpec((width, 512), column),
            ],
            out_specs=[
                pl.BlockSpec((IMG, width), lambda i, place: (0, 0)),
                pl.BlockSpec((1, IMG_TALL, 256), lambda i, place: (i, 0, 0)),
                pl.BlockSpec((1, IMG_TALL, 256), lambda i, place: (i, 0, 0)),
            ],
            scratch_shapes=[pltpu.VMEM((IMG, width), BF), pltpu.VMEM((16, 256), BF)],
        ),
        out_shape=[jax.ShapeDtypeStruct((IMG, width), BF), out, out],
        compiler_params=pltpu.CompilerParams(vmem_limit_bytes=VMEM_LIMIT),
        cost_estimate=LIGHT,
        name="image_rows_kv",
    )(place, pieces, bias, gain, kv_w)


def close_kernel(a_ref, b_ref, c_ref, d_ref, labels_ref, out_ref):
    total = a_ref[...].astype(F32) + b_ref[...].astype(F32)
    total = total + c_ref[...].astype(F32) + d_ref[...].astype(F32)
    squares = total[IMG : IMG + 1, 0:128] + total[IMG + 1 : IMG + 2, 0:128]
    scale = lax.rsqrt(squares / D + 1e-05)
    scale = jnp.where(labels_ref[3:4, 0:128].astype(F32) > 0.5, scale, 0.0)
    tile = jnp.broadcast_to(scale, (128, 128)).T[0:IMG]
    tile = jnp.concatenate([tile, tile], axis=1)
    out_ref[0:IMG, :] = jnp.where(tile > 0.0, total[0:IMG] * tile, 0.0).astype(BF)
    out_ref[IMG:, :] = labels_ref[...]


def close_images(parts, labels):
    return pl.pallas_call(
        close_kernel,
        out_shape=jax.ShapeDtypeStruct((IMG_TALL, 256), BF),
        cost_estimate=LIGHT,
        name="close_images",
    )(*parts, labels)


def merge_kernel(
    place,
    slots,
    own_near,
    own_far,
    rows_ref,
    key_near,
    value_near,
    key_far,
    value_far,
    near_ref,
    side_ref,
    yonder_ref,
    far_ref,
    out_ref,
    placed,
):
    prefill = place[0] == 0
    step = pl.program_id(0)
    here, there = place[3] // 4, 1 - place[3] // 4
    level = lax.rem(place[3] + 8 - step, 4)

    @pl.when(jnp.logical_and(prefill, step == 0))
    def _():
        placed[...] = jnp.zeros_like(placed)
        for p in range(PAGES):
            placed[slots[p]] = rows_ref[p]

    spots = lax.broadcasted_iota(jnp.int32, (CAP * PAGE, 2 * IMG), 0).astype(F32)

    def one(images, owner, upper, left, right):
        targets = []
        for image in images:
            labels = image[0, IMG:IMG_TALL, 0:IMG].astype(F32)
            spot = labels[1:2] * PAGE + labels[2:3]
            targets.append(jnp.where(labels[0:1] == owner.astype(F32), spot, -1.0))
        target = jnp.concatenate(targets, axis=1)
        data = jnp.concatenate([images[0][0, 0:IMG, :], images[1][0, 0:IMG, :]], axis=0)
        chosen = (spots == target).astype(F32).astype(BF)
        image = jnp.dot(chosen, data, preferred_element_type=F32).astype(BF)
        for half, text in enumerate((left, right)):
            lanes = slice(half * 128, half * 128 + 128)
            merged = text.reshape(CAP * PAGE, 128) + image[:, lanes]
            out_ref[upper, 0, :, :, lanes] = merged.reshape(CAP, PAGE, 128)

    @pl.when(prefill)
    def _():
        for own_ref, upper in ((own_near, here), (own_far, there)):
            owner = upper * 4 + level
            one((near_ref, side_ref), owner, upper, own_ref[0], placed[pl.ds(owner * CAP, CAP)])

    @pl.when(jnp.logical_not(prefill))
    def _():
        one((near_ref, side_ref), place[3], here, key_near[0], value_near[0])
        one((yonder_ref, far_ref), place[3], there, key_far[0], value_far[0])


def merge_slots(place, slots, own, rows, arrived, images):
    def level(i, place):
        return lax.rem(place[3] + 8 - i, 4)

    def chunk(base, apart, prefill):
        def index(i, place, slots):
            y = place[3] // 4
            y = 1 - y if apart else y
            used = (place[0] == 0) == prefill
            return (base + jnp.where(used, 4 * y + level(i, place), 0), 0, 0, 0)

        return pl.BlockSpec((1, CAP, PAGE, 128), index)

    image_spec = pl.BlockSpec(
        (1, IMG_TALL, 256), lambda i, place, slots: (jnp.where(place[0] == 0, 0, i), 0, 0)
    )
    own = own.reshape(16, CAP, PAGE, 128)
    arrived = arrived.reshape(16, CAP, PAGE, 128)
    near, yonder, side, far = images
    result = pl.pallas_call(
        merge_kernel,
        grid_spec=pltpu.PrefetchScalarGridSpec(
            num_scalar_prefetch=2,
            grid=(4,),
            in_specs=[
                chunk(8, False, True),
                chunk(8, True, True),
                pl.BlockSpec((PAGES, PAGE, 128), lambda i, place, slots: (0, 0, 0)),
                chunk(0, False, False),
                chunk(8, False, False),
                chunk(0, True, False),
                chunk(8, True, False),
            ]
            + [image_spec] * 4,
            out_specs=pl.BlockSpec(
                (2, 1, CAP, PAGE, 256), lambda i, place, slots: (0, level(i, place), 0, 0, 0)
            ),
            scratch_shapes=[pltpu.VMEM((256, PAGE, 128), BF)],
        ),
        out_shape=jax.ShapeDtypeStruct((2, 4, CAP, PAGE, 256), BF),
        compiler_params=pltpu.CompilerParams(vmem_limit_bytes=VMEM_LIMIT),
        cost_estimate=LIGHT,
        name="merge_slots",
    )(place, slots, own, own, rows, arrived, arrived, arrived, arrived, near, side, yonder, far)
    return result.reshape(256, PAGE, 256)


def attend(queries, kv_cache, new_kv, cache_lengths):
    row_count = queries.shape[0]
    heads_kv = kv_cache.shape[2] // (2 * HEAD)
    grouped = queries.reshape(row_count, heads_kv, queries.shape[1] // (HEAD * heads_kv), HEAD)
    stored = kv_cache.reshape(row_count, kv_cache.shape[1], heads_kv, 2 * HEAD)
    fresh_kv = new_kv.reshape(row_count, heads_kv, 2 * HEAD)
    scores = jnp.einsum(
        "rgqh,rjgh->rgqj", grouped, stored[..., :HEAD], preferred_element_type=jnp.float32
    ) * HEAD ** (-0.5)
    in_cache = jnp.arange(stored.shape[1], dtype=jnp.int32)[None, :] < cache_lengths[:, None]
    scores = jnp.where(in_cache[:, None, None, :], scores, -1e30)
    own_score = jnp.einsum(
        "rgqh,rgh->rgq", grouped, fresh_kv[..., :HEAD], preferred_element_type=jnp.float32
    ) * HEAD ** (-0.5)
    row_max = jnp.maximum(jnp.max(scores, axis=3), own_score)
    weights = jnp.exp(scores - row_max[..., None])
    own_weight = jnp.exp(own_score - row_max)
    denominator = jnp.sum(weights, axis=3) + own_weight
    probability = (weights / denominator[..., None]).astype(jnp.bfloat16)
    own_prob = lax.optimization_barrier((own_weight / denominator).astype(jnp.bfloat16)).astype(
        jnp.float32
    )
    attended = jnp.einsum(
        "rgqj,rjgh->rgqh", probability, stored[..., HEAD:], preferred_element_type=jnp.float32
    )
    attended = attended + own_prob[..., None] * fresh_kv[:, :, None, HEAD:].astype(jnp.float32)
    return attended.astype(jnp.bfloat16).reshape(row_count, queries.shape[1])


PARTNER = [(i, i ^ 1) for i in range(8)]


def shift(k):
    return [(i, (i + 2 * k) % 8) for i in range(8)]


def seq_shift(y, z):
    return [(i, (i // 4 + y) % 2 * 4 + (i + z) % 4) for i in range(8)]


FAR = [(i, 8 + (i + 4) % 8) for i in range(8)]
AWAY = [(8 + i, 8 + (i + 4) % 8) for i in range(8)]


def after(value, other):
    return lax.optimization_barrier((value, other))[0]


def per_device(
    embeds,
    image_feats,
    image_pos,
    proj_w,
    proj_b,
    norm_gain,
    kv_w,
    prompt_lengths,
    page_owner,
    queries,
    kv_cache,
    new_kv,
    cache_lengths,
):
    group = lax.axis_index("group").astype(jnp.int32)
    seq = lax.axis_index("seq").astype(jnp.int32)
    mp = lax.axis_index("mp").astype(jnp.int32)
    core, x = mp % 2, mp // 2
    place = jnp.stack([group, core, x, seq])


    owners = page_owner[:, 0]
    before = (
        jnp.arange(PAGES, dtype=jnp.int32)[None, :] < jnp.arange(PAGES, dtype=jnp.int32)[:, None]
    )
    page_rank = jnp.sum((before & (owners[:, None] == owners[None, :])).astype(jnp.int32), axis=1)
    slots = owners * CAP + page_rank
    live = jnp.sum(jnp.where(jnp.arange(4, dtype=jnp.int32) == seq // 2, prompt_lengths, 0))
    limit = live - (seq % 2) * ROWS
    local_pos = lax.dynamic_slice(image_pos, (group * IMG,), (IMG,)) - seq * ROWS
    at_page = (local_pos // PAGE)[:, None] == jnp.arange(PAGES, dtype=jnp.int32)[None, :]
    image_owner = jnp.sum(jnp.where(at_page, owners[None, :], 0), axis=1)
    image_rank = jnp.sum(jnp.where(at_page, page_rank[None, :], 0), axis=1)
    labels = jnp.stack(
        [image_owner, image_rank, local_pos % PAGE, (local_pos < limit).astype(jnp.int32)]
    ).astype(BF)
    tokens = jnp.arange(ROWS, dtype=jnp.int32).reshape(16, 128)
    places = image_pos - seq * ROWS
    upper = (places // 128)[None, :] == jnp.arange(16, dtype=jnp.int32)[:, None]
    lower = (places % 128)[:, None] == jnp.arange(128, dtype=jnp.int32)[None, :]
    is_image = jnp.dot(upper.astype(BF), lower.astype(BF), preferred_element_type=F32)
    mask = jnp.where((tokens < limit) & (is_image < 0.5), 1.0, 0.0).astype(F32)
    labels = jnp.pad(labels, ((0, 12), (0, 256 - IMG)))

    got = lax.all_to_all(cut_features(place, image_feats), "seq", 0, 0, tiled=True)

    send, keep = project_text(place, embeds, norm_gain, kv_w)
    got = after(got, keep[0])
    swapped = lax.ppermute(got, "mp", PARTNER)
    received = [lax.ppermute(piece, "mp", PARTNER) for piece in send]
    added = [None] + [add_pair(keep[j], received[j]) for j in (1, 2, 3)]
    parts = [keep[0], received[0]] + [lax.ppermute(added[j], "mp", shift(j)) for j in (1, 2, 3)]

    feats = jnp.concatenate([got, after(swapped, added[1:])], axis=1).reshape(8 * IMG, -1)
    partial = jnp.dot(feats, proj_w, preferred_element_type=F32).astype(BF).reshape(8, IMG, -1)
    attended = lax.cond(
        group != 0,
        attend,
        lambda *unused: jnp.zeros(queries.shape, BF),
        after(queries, partial),
        kv_cache,
        new_kv,
        cache_lengths,
    )
    pieces = lax.all_to_all(partial, "seq", 0, 0, tiled=True)
    image_hidden, swap, same = image_rows_kv(place, pieces, proj_b, norm_gain, kv_w)
    image_pairs = add_pair(same, lax.ppermute(swap, "mp", PARTNER))
    image_parts = [image_pairs[0]]
    image_parts += [lax.ppermute(image_pairs[j], "mp", shift(j)) for j in (1, 2, 3)]

    rows, by_owner = finish_text(slots, after(mask, attended), parts)
    other_rows = lax.ppermute(rows, "group", [(1, 0)])
    arrived = lax.all_to_all(
        by_owner.reshape(512, PAGE, 128), ("group", "seq"), split_axis=0, concat_axis=0, tiled=True
    ).reshape(2, 256, PAGE, 128)

    image_parts = after(image_parts, by_owner)
    image_block = close_images(image_parts, labels)
    near = jnp.stack(
        [image_block] + [lax.ppermute(image_block, "seq", seq_shift(0, k)) for k in (1, 2, 3)]
    )
    images = [
        near,
        lax.ppermute(near, ("group", "seq"), AWAY),
        lax.ppermute(near, "group", [(0, 1), (1, 0)]),
        lax.ppermute(near, ("group", "seq"), FAR),
    ]
    page_slots = merge_slots(place, slots, by_owner, other_rows, arrived, images)

    other_hidden = lax.ppermute(image_hidden, "group", [(1, 0)])
    row_states = jnp.where(
        group == 0, jnp.concatenate([image_hidden, other_hidden], axis=0), attended
    )
    return (page_slots, row_states)


def solution(mesh):
    in_specs = (
        P("seq", "mp"),
        P("seq", None),
        P("seq"),
        P("seq", "mp"),
        P("mp"),
        P("mp"),
        P("mp", None),
        P(),
        P("seq", None),
        P("seq", "mp"),
        P("seq", None, "mp"),
        P("seq", "mp"),
        P("seq"),
    )
    out_specs = (P(("group", "seq"), None, "mp"), P(("group", "seq"), "mp"))
    return jax.shard_map(
        per_device, mesh=mesh, in_specs=in_specs, out_specs=out_specs, check_vma=False
    )
```

```python
import functools

import jax
import jax.numpy as jnp
from jax import lax
from jax.experimental import pallas as pl
from jax.experimental.pallas import tpu as pltpu
from jax.sharding import PartitionSpec as P

D = 8192
HEAD = 128
PAGE = 16
PROMPT_LEN = 4096
CAP = 32
ROWS = 2048
EXT = 32
TALL = ROWS + EXT
PAGES = ROWS // PAGE
IMG = 64
IMG_TALL = IMG + 16
BF = jnp.bfloat16
F32 = jnp.float32
def work(micros):
    size = int(micros * 3700000)
    return pl.CostEstimate(flops=micros * 1000000, bytes_accessed=size, transcendentals=0)


LIGHT = pl.CostEstimate(flops=1, bytes_accessed=1, transcendentals=0)
VMEM_LIMIT = 56 * 1024 * 1024


def split_pair(value):
    high = value.astype(BF)
    low = (value - high.astype(F32)).astype(BF)
    return high, low


TILE = 512
STEPS = ROWS // TILE


def project_kernel(place, embeds_ref, gain_ref, *refs):
    weights, send, keep, squares_ref = refs[0:8], refs[8:12], refs[12:16], refs[16]
    step = pl.program_id(0)

    @pl.when(step < STEPS)
    def _():
        hidden = embeds_ref[...].astype(F32)
        scaled = (hidden * gain_ref[...].astype(F32).reshape(1, -1)).astype(BF)
        squared = hidden * hidden
        lanes = squared[:, 0:128]
        for k in range(1, 8):
            lanes = lanes + squared[:, k * 128 : (k + 1) * 128]
        summed = jnp.sum(lanes.T, axis=0, keepdims=True)
        for k in range(TILE // 128):
            squares_ref[pl.ds(TILE // 128 * step + k, 1), :] = summed[:, k * 128 : (k + 1) * 128]
        for k, target in enumerate((send[:2], send[2:], keep[:2], keep[2:])):
            weight = jnp.concatenate([weights[2 * k][...], weights[2 * k + 1][...]], axis=1)
            product = jnp.dot(scaled, weight, preferred_element_type=F32).astype(BF)
            target[0][...] = product[:, :128]
            target[1][...] = product[:, 128:]

    @pl.when(step == STEPS)
    def _():
        high, low = split_pair(squares_ref[...])
        both = jnp.concatenate([high, low], axis=0)
        for ref in (*send, *keep):
            ref[0:EXT, :] = both


def project_text(place, embeds, gain, kv_w):
    def column(r, j):
        def index(i, place):
            core = place[1] if r else 1 - place[1]
            head = 2 * lax.rem(place[2] + j, 4) + core
            return (0, 2 * head + place[0])

        return index

    specs = [
        pl.BlockSpec((TILE, 1024), lambda i, place: (jnp.minimum(i, STEPS - 1), 0)),
        pl.BlockSpec((1024,), lambda i, place: (0,)),
    ] + [pl.BlockSpec((1024, 128), column(r, j)) for r in range(2) for j in range(4)]
    outs = pl.pallas_call(
        project_kernel,
        grid_spec=pltpu.PrefetchScalarGridSpec(
            num_scalar_prefetch=1,
            grid=(STEPS + 1,),
            in_specs=specs,
            out_specs=[pl.BlockSpec((TILE, 128), lambda i, place: (i, 0))] * 8,
            scratch_shapes=[pltpu.VMEM((16, 128), F32)],
        ),
        out_shape=[jax.ShapeDtypeStruct((TALL, 128), BF)] * 8,
        compiler_params=pltpu.CompilerParams(vmem_limit_bytes=VMEM_LIMIT),
        cost_estimate=LIGHT,
        name="project_text",
    )(place, embeds, gain, *([kv_w] * 8))
    return outs[:4], outs[4:]


def square_rows(refs):
    total = jnp.zeros((16, 128), F32)
    for ref in refs:
        total = total + ref[ROWS : ROWS + 16, :].astype(F32) + ref[ROWS + 16 : TALL, :].astype(F32)
    return total


def add_pair(keep, received):
    return (keep.astype(F32) + received.astype(F32)).astype(BF)


def finish_kernel(slots, mask_ref, *refs):
    parts, (rows_ref, slot_ref) = refs[:5], refs[5:]
    slot_ref[...] = jnp.zeros_like(slot_ref)
    squares = square_rows(parts)
    scale = jnp.where(mask_ref[...] > 0.0, lax.rsqrt(squares / D + 1e-05), 0.0)
    for part in range(16):
        tile = jnp.broadcast_to(scale[part : part + 1, :], (128, 128)).T
        here = slice(part * 128, part * 128 + 128)
        total = parts[0][here, :].astype(F32)
        for ref in parts[1:]:
            total = total + ref[here, :].astype(F32)
        rows = jnp.where(tile > 0.0, total * tile, 0.0).astype(BF)
        for p in range(8):
            page = rows[p * PAGE : (p + 1) * PAGE, :]
            rows_ref[part * 8 + p] = page
            slot_ref[0, slots[part * 8 + p]] = page


def finish_text(slots, mask, parts):
    whole = lambda i, slots: (0, 0)
    return pl.pallas_call(
        finish_kernel,
        grid_spec=pltpu.PrefetchScalarGridSpec(
            num_scalar_prefetch=1,
            grid=(1,),
            in_specs=[pl.BlockSpec((16, 128), whole)] + [pl.BlockSpec((TALL, 128), whole)] * 5,
            out_specs=[
                pl.BlockSpec((PAGES, PAGE, 128), lambda i, slots: (0, 0, 0)),
                pl.BlockSpec((1, 256, PAGE, 128), lambda i, slots: (1, 0, 0, 0)),
            ],
        ),
        out_shape=[
            jax.ShapeDtypeStruct((PAGES, PAGE, 128), BF),
            jax.ShapeDtypeStruct((2, 256, PAGE, 128), BF),
        ],
        compiler_params=pltpu.CompilerParams(vmem_limit_bytes=VMEM_LIMIT),
        cost_estimate=work(20000),
        name="finish_text",
    )(slots, mask, *parts)


def cut_kernel(place, feats_ref, out_ref):
    depth = out_ref.shape[2]
    for k in range(8):
        out_ref[k] = feats_ref[:, k * depth : (k + 1) * depth]


def cut_features(place, feats):
    depth = feats.shape[1] // 8
    return pl.pallas_call(
        cut_kernel,
        grid_spec=pltpu.PrefetchScalarGridSpec(
            num_scalar_prefetch=1,
            grid=(1,),
            in_specs=[
                pl.BlockSpec((32, feats.shape[1]), lambda i, place: (2 * place[0] + place[1], 0))
            ],
            out_specs=pl.BlockSpec((8, 32, depth), lambda i, place: (0, 0, 0)),
        ),
        out_shape=jax.ShapeDtypeStruct((8, 32, depth), BF),
        cost_estimate=LIGHT,
        name="cut_features",
    )(place, feats)


def image_kernel(
    place, pieces_ref, bias_ref, gain_ref, weight_ref, other_ref, hidden_ref, swap_ref, same_ref, scaled, pair
):
    step = pl.program_id(0)

    @pl.when(step == 0)
    def _():
        total = pieces_ref[0].astype(F32)
        for k in range(1, 8):
            total = total + pieces_ref[k].astype(F32)
        flipped = jnp.concatenate([total[32:64], total[0:32]], axis=0)
        total = jnp.where(place[1] == 0, total, flipped)
        total = total + bias_ref[...].astype(F32).reshape(1, -1)
        image_hidden = (0.5 * total * (1.0 + lax.erf(total * (0.5**0.5)))).astype(BF)
        hidden_ref[...] = image_hidden
        hidden = image_hidden.astype(F32)
        scaled[...] = (hidden * gain_ref[...].astype(F32).reshape(1, -1)).astype(BF)
        squared = hidden * hidden
        lanes = squared[:, 0:128]
        for k in range(1, 8):
            lanes = lanes + squared[:, k * 128 : (k + 1) * 128]
        lanes = jnp.concatenate([lanes, jnp.zeros_like(lanes)], axis=0)
        summed = jnp.sum(lanes.T, axis=0, keepdims=True)
        high, low = split_pair(summed)
        picked = lax.broadcasted_iota(jnp.int32, (16, 128), 0)
        rows = jnp.where(picked == 0, high.astype(F32), jnp.where(picked == 1, low.astype(F32), 0.0))
        pair[...] = jnp.concatenate([rows, jnp.zeros_like(rows)], axis=1).astype(BF)

    first = place[1] == 0
    for k, weight in enumerate((weight_ref, other_ref)):
        product = jnp.dot(scaled[...], weight[...], preferred_element_type=F32)
        left, right = product[:, :256], product[:, 256:]
        same_ref[k, 0:IMG, :] = jnp.where(first, left, right).astype(BF)
        swap_ref[k, 0:IMG, :] = jnp.where(first, right, left).astype(BF)
        same_ref[k, IMG:, :] = pair[...]
        swap_ref[k, IMG:, :] = pair[...]


def image_rows_kv(place, pieces, bias, gain, kv_w):
    def column(k):
        return lambda i, place: (0, lax.rem(place[2] + 2 * i + k, 4))

    width = pieces.shape[2]
    row = pl.BlockSpec((width,), lambda i, place: (0,))
    out = jax.ShapeDtypeStruct((4, IMG_TALL, 256), BF)
    return pl.pallas_call(
        image_kernel,
        grid_spec=pltpu.PrefetchScalarGridSpec(
            num_scalar_prefetch=1,
            grid=(2,),
            in_specs=[
                pl.BlockSpec((8, IMG, width), lambda i, place: (0, 0, 0)),
                row,
                row,
                pl.BlockSpec((width, 512), column(0)),
                pl.BlockSpec((width, 512), column(1)),
            ],
            out_specs=[
                pl.BlockSpec((IMG, width), lambda i, place: (0, 0)),
                pl.BlockSpec((2, IMG_TALL, 256), lambda i, place: (i, 0, 0)),
                pl.BlockSpec((2, IMG_TALL, 256), lambda i, place: (i, 0, 0)),
            ],
            scratch_shapes=[pltpu.VMEM((IMG, width), BF), pltpu.VMEM((16, 256), BF)],
        ),
        out_shape=[jax.ShapeDtypeStruct((IMG, width), BF), out, out],
        compiler_params=pltpu.CompilerParams(vmem_limit_bytes=VMEM_LIMIT),
        cost_estimate=LIGHT,
        name="image_rows_kv",
    )(place, pieces, bias, gain, kv_w, kv_w)


def close_kernel(a_ref, b_ref, c_ref, d_ref, labels_ref, out_ref):
    total = a_ref[...].astype(F32) + b_ref[...].astype(F32)
    total = total + c_ref[...].astype(F32) + d_ref[...].astype(F32)
    squares = total[IMG : IMG + 1, 0:128] + total[IMG + 1 : IMG + 2, 0:128]
    scale = lax.rsqrt(squares / D + 1e-05)
    scale = jnp.where(labels_ref[3:4, 0:128].astype(F32) > 0.5, scale, 0.0)
    tile = jnp.broadcast_to(scale, (128, 128)).T[0:IMG]
    tile = jnp.concatenate([tile, tile], axis=1)
    out_ref[0:IMG, :] = jnp.where(tile > 0.0, total[0:IMG] * tile, 0.0).astype(BF)
    out_ref[IMG:, :] = labels_ref[...]


def close_images(parts, labels):
    return pl.pallas_call(
        close_kernel,
        out_shape=jax.ShapeDtypeStruct((IMG_TALL, 256), BF),
        cost_estimate=LIGHT,
        name="close_images",
    )(*parts, labels)


def merge_kernel(
    place,
    slots,
    own_near,
    own_far,
    rows_ref,
    key_near,
    value_near,
    key_far,
    value_far,
    near_ref,
    side_ref,
    yonder_ref,
    far_ref,
    out_ref,
    placed,
):
    prefill = place[0] == 0
    step = pl.program_id(0)
    here, there = place[3] // 4, 1 - place[3] // 4
    level = lax.rem(place[3] + 8 - step, 4)

    @pl.when(jnp.logical_and(prefill, step == 0))
    def _():
        placed[...] = jnp.zeros_like(placed)
        for p in range(PAGES):
            placed[slots[p]] = rows_ref[p]

    spots = lax.broadcasted_iota(jnp.int32, (CAP * PAGE, 2 * IMG), 0).astype(F32)

    def one(images, owner, upper, left, right):
        targets = []
        for image in images:
            labels = image[0, IMG:IMG_TALL, 0:IMG].astype(F32)
            spot = labels[1:2] * PAGE + labels[2:3]
            targets.append(jnp.where(labels[0:1] == owner.astype(F32), spot, -1.0))
        target = jnp.concatenate(targets, axis=1)
        data = jnp.concatenate([images[0][0, 0:IMG, :], images[1][0, 0:IMG, :]], axis=0)
        chosen = (spots == target).astype(F32).astype(BF)
        image = jnp.dot(chosen, data, preferred_element_type=F32).astype(BF)
        for half, text in enumerate((left, right)):
            lanes = slice(half * 128, half * 128 + 128)
            merged = text.reshape(CAP * PAGE, 128) + image[:, lanes]
            out_ref[upper, 0, :, :, lanes] = merged.reshape(CAP, PAGE, 128)

    @pl.when(prefill)
    def _():
        for own_ref, upper in ((own_near, here), (own_far, there)):
            owner = upper * 4 + level
            one((near_ref, side_ref), owner, upper, own_ref[0], placed[pl.ds(owner * CAP, CAP)])

    @pl.when(jnp.logical_not(prefill))
    def _():
        one((near_ref, side_ref), place[3], here, key_near[0], value_near[0])
        one((yonder_ref, far_ref), place[3], there, key_far[0], value_far[0])


def merge_slots(place, slots, own, rows, arrived, images):
    def level(i, place):
        return lax.rem(place[3] + 8 - i, 4)

    def chunk(base, apart, prefill):
        def index(i, place, slots):
            y = place[3] // 4
            y = 1 - y if apart else y
            used = (place[0] == 0) == prefill
            return (base + jnp.where(used, 4 * y + level(i, place), 0), 0, 0, 0)

        return pl.BlockSpec((1, CAP, PAGE, 128), index)

    image_spec = pl.BlockSpec(
        (1, IMG_TALL, 256), lambda i, place, slots: (jnp.where(place[0] == 0, 0, i), 0, 0)
    )
    own = own.reshape(16, CAP, PAGE, 128)
    arrived = arrived.reshape(16, CAP, PAGE, 128)
    near, yonder, side, far = images
    result = pl.pallas_call(
        merge_kernel,
        grid_spec=pltpu.PrefetchScalarGridSpec(
            num_scalar_prefetch=2,
            grid=(4,),
            in_specs=[
                chunk(8, False, True),
                chunk(8, True, True),
                pl.BlockSpec((PAGES, PAGE, 128), lambda i, place, slots: (0, 0, 0)),
                chunk(0, False, False),
                chunk(8, False, False),
                chunk(0, True, False),
                chunk(8, True, False),
            ]
            + [image_spec] * 4,
            out_specs=pl.BlockSpec(
                (2, 1, CAP, PAGE, 256), lambda i, place, slots: (0, level(i, place), 0, 0, 0)
            ),
            scratch_shapes=[pltpu.VMEM((256, PAGE, 128), BF)],
        ),
        out_shape=jax.ShapeDtypeStruct((2, 4, CAP, PAGE, 256), BF),
        compiler_params=pltpu.CompilerParams(vmem_limit_bytes=VMEM_LIMIT),
        cost_estimate=LIGHT,
        name="merge_slots",
    )(place, slots, own, own, rows, arrived, arrived, arrived, arrived, near, side, yonder, far)
    return result.reshape(256, PAGE, 256)


def attend(queries, kv_cache, new_kv, cache_lengths):
    row_count = queries.shape[0]
    heads_kv = kv_cache.shape[2] // (2 * HEAD)
    grouped = queries.reshape(row_count, heads_kv, queries.shape[1] // (HEAD * heads_kv), HEAD)
    stored = kv_cache.reshape(row_count, kv_cache.shape[1], heads_kv, 2 * HEAD)
    fresh_kv = new_kv.reshape(row_count, heads_kv, 2 * HEAD)
    scores = jnp.einsum(
        "rgqh,rjgh->rgqj", grouped, stored[..., :HEAD], preferred_element_type=jnp.float32
    ) * HEAD ** (-0.5)
    in_cache = jnp.arange(stored.shape[1], dtype=jnp.int32)[None, :] < cache_lengths[:, None]
    scores = jnp.where(in_cache[:, None, None, :], scores, -1e30)
    own_score = jnp.einsum(
        "rgqh,rgh->rgq", grouped, fresh_kv[..., :HEAD], preferred_element_type=jnp.float32
    ) * HEAD ** (-0.5)
    row_max = jnp.maximum(jnp.max(scores, axis=3), own_score)
    weights = jnp.exp(scores - row_max[..., None])
    own_weight = jnp.exp(own_score - row_max)
    denominator = jnp.sum(weights, axis=3) + own_weight
    probability = (weights / denominator[..., None]).astype(jnp.bfloat16)
    own_prob = lax.optimization_barrier((own_weight / denominator).astype(jnp.bfloat16)).astype(
        jnp.float32
    )
    attended = jnp.einsum(
        "rgqj,rjgh->rgqh", probability, stored[..., HEAD:], preferred_element_type=jnp.float32
    )
    attended = attended + own_prob[..., None] * fresh_kv[:, :, None, HEAD:].astype(jnp.float32)
    return attended.astype(jnp.bfloat16).reshape(row_count, queries.shape[1])


PARTNER = [(i, i ^ 1) for i in range(8)]


def shift(k):
    return [(i, (i + 2 * k) % 8) for i in range(8)]


def seq_shift(y, z):
    return [(i, (i // 4 + y) % 2 * 4 + (i + z) % 4) for i in range(8)]


FAR = [(i, 8 + (i + 4) % 8) for i in range(8)]
AWAY = [(8 + i, 8 + (i + 4) % 8) for i in range(8)]


def after(value, other):
    return lax.optimization_barrier((value, other))[0]


def per_device(
    embeds,
    image_feats,
    image_pos,
    proj_w,
    proj_b,
    norm_gain,
    kv_w,
    prompt_lengths,
    page_owner,
    queries,
    kv_cache,
    new_kv,
    cache_lengths,
):
    group = lax.axis_index("group").astype(jnp.int32)
    seq = lax.axis_index("seq").astype(jnp.int32)
    mp = lax.axis_index("mp").astype(jnp.int32)
    core, x = mp % 2, mp // 2
    place = jnp.stack([group, core, x, seq])


    owners = page_owner[:, 0]
    before = (
        jnp.arange(PAGES, dtype=jnp.int32)[None, :] < jnp.arange(PAGES, dtype=jnp.int32)[:, None]
    )
    page_rank = jnp.sum((before & (owners[:, None] == owners[None, :])).astype(jnp.int32), axis=1)
    slots = owners * CAP + page_rank
    live = jnp.sum(jnp.where(jnp.arange(4, dtype=jnp.int32) == seq // 2, prompt_lengths, 0))
    limit = live - (seq % 2) * ROWS
    local_pos = lax.dynamic_slice(image_pos, (group * IMG,), (IMG,)) - seq * ROWS
    at_page = (local_pos // PAGE)[:, None] == jnp.arange(PAGES, dtype=jnp.int32)[None, :]
    image_owner = jnp.sum(jnp.where(at_page, owners[None, :], 0), axis=1)
    image_rank = jnp.sum(jnp.where(at_page, page_rank[None, :], 0), axis=1)
    labels = jnp.stack(
        [image_owner, image_rank, local_pos % PAGE, (local_pos < limit).astype(jnp.int32)]
    ).astype(BF)
    tokens = jnp.arange(ROWS, dtype=jnp.int32).reshape(16, 128)
    places = image_pos - seq * ROWS
    upper = (places // 128)[None, :] == jnp.arange(16, dtype=jnp.int32)[:, None]
    lower = (places % 128)[:, None] == jnp.arange(128, dtype=jnp.int32)[None, :]
    is_image = jnp.dot(upper.astype(BF), lower.astype(BF), preferred_element_type=F32)
    mask = jnp.where((tokens < limit) & (is_image < 0.5), 1.0, 0.0).astype(F32)
    labels = jnp.pad(labels, ((0, 12), (0, 256 - IMG)))

    got = lax.all_to_all(cut_features(place, image_feats), "seq", 0, 0, tiled=True)

    send, keep = project_text(place, embeds, norm_gain, kv_w)
    got = after(got, keep[0])
    swapped = lax.ppermute(got, "mp", PARTNER)
    received = [lax.ppermute(piece, "mp", PARTNER) for piece in send]
    added = [None] + [add_pair(keep[j], received[j]) for j in (1, 2, 3)]
    parts = [keep[0], received[0]] + [lax.ppermute(added[j], "mp", shift(j)) for j in (1, 2, 3)]

    feats = jnp.concatenate([got, after(swapped, added[1:])], axis=1).reshape(8 * IMG, -1)
    partial = jnp.dot(feats, proj_w, preferred_element_type=F32).astype(BF).reshape(8, IMG, -1)
    attended = lax.cond(
        group != 0,
        attend,
        lambda *unused: jnp.zeros(queries.shape, BF),
        after(queries, partial),
        kv_cache,
        new_kv,
        cache_lengths,
    )
    pieces = lax.all_to_all(partial, "seq", 0, 0, tiled=True)
    image_hidden, swap, same = image_rows_kv(place, pieces, proj_b, norm_gain, kv_w)
    image_pairs = add_pair(same, lax.ppermute(swap, "mp", PARTNER))
    image_parts = [image_pairs[0]]
    image_parts += [lax.ppermute(image_pairs[j], "mp", shift(j)) for j in (1, 2, 3)]

    rows, by_owner = finish_text(slots, after(mask, attended), parts)
    other_rows = lax.ppermute(rows, "group", [(1, 0)])
    arrived = lax.all_to_all(
        by_owner.reshape(512, PAGE, 128), ("group", "seq"), split_axis=0, concat_axis=0, tiled=True
    ).reshape(2, 256, PAGE, 128)

    image_parts = after(image_parts, by_owner)
    image_block = close_images(image_parts, labels)
    near = jnp.stack(
        [image_block] + [lax.ppermute(image_block, "seq", seq_shift(0, k)) for k in (1, 2, 3)]
    )
    images = [
        near,
        lax.ppermute(near, ("group", "seq"), AWAY),
        lax.ppermute(near, "group", [(0, 1), (1, 0)]),
        lax.ppermute(near, ("group", "seq"), FAR),
    ]
    page_slots = merge_slots(place, slots, by_owner, other_rows, arrived, images)

    other_hidden = lax.ppermute(image_hidden, "group", [(1, 0)])
    row_states = jnp.where(
        group == 0, jnp.concatenate([image_hidden, other_hidden], axis=0), attended
    )
    return (page_slots, row_states)


def solution(mesh):
    in_specs = (
        P("seq", "mp"),
        P("seq", None),
        P("seq"),
        P("seq", "mp"),
        P("mp"),
        P("mp"),
        P("mp", None),
        P(),
        P("seq", None),
        P("seq", "mp"),
        P("seq", None, "mp"),
        P("seq", "mp"),
        P("seq"),
    )
    out_specs = (P(("group", "seq"), None, "mp"), P(("group", "seq"), "mp"))
    return jax.shard_map(
        per_device, mesh=mesh, in_specs=in_specs, out_specs=out_specs, check_vma=False
    )
```
